128 devices in a mesh: row: 8 (over x, core), col: 16 (over y, z).
Axes of the slice: x: 4, y: 4, z: 4, core: 2. Of those that a mesh axis runs over, the one named last changes fastest.
Arguments:
- response_cache: bfloat16 [256, 256, 256], P('col'), may hold values from -128 to 128
- near_cache: bfloat16 [8, 256, 256], replicated, may hold values from -0.0073296421 to 0.0073296421
- lead_diag: float32 [512], replicated, may hold values from 0.25 to 2
- far_offsets: int32 [512, 24], P(('row', 'col')), may hold values from 0 to 255, as said below
- near_first: int32 [512, 24], P(('row', 'col')), may hold values from 0 to 7
- near_second: int32 [512, 24], P(('row', 'col')), may hold values from 0 to 7
- tile_counts: int32 [512], P(('row', 'col')), may hold values from 1 to 24, as said below
Outputs:
- lead_factor: float32 [512, 512], replicated
- far_factor: float32 [131072, 512], P(('row', 'col'))
The draws below stay inside these ranges and needn't reach their ends.
Inputs may be any that keep to these rules, and one draw needn't show every extreme that they name: Slots at positions tile_counts[f] and above are unused; the last far tile uses all 24 slots. Among the slots of the 4 far tiles of one device, at most 8 have far_offsets // 16 equal to any one value, and exactly 8 for some value.
All inputs are finite; a program needn't handle non-finite values.
Results may differ from the reference program's by a relative error of at most 0.0003.
Values may be sent and summed in bfloat16 or wider, within the bound.
No kernel may reach another device: no remote copies, remote signals or barrier semaphores. Data moves between devices by JAX's collectives and lax.ppermute only.
A program may use at most 192 MiB of HBM per device.

```python
import math
import jax
import jax.numpy as jnp
from jax import lax

TILE = 256
NNEAR = 8
CAP = 24
RESP_DEV = 16
TILES_DEV = 4
FAR_TILES = 512
NRESP = 256
MOST = 8
N_COL = 16
DEVICES = 128


def draw_tile_counts(key, part):
    positions = jnp.arange(FAR_TILES, dtype=jnp.int32)
    low_top = max(CAP // 3, 1)
    highest = low_top + positions * (CAP - low_top) // max(FAR_TILES - 1, 1)
    lowest = jnp.maximum(highest // 2, 1)
    raw_bits = jax.random.randint(key, (FAR_TILES,), 0, 1 << 20)
    counts = lowest + raw_bits % (highest - lowest + 1)
    return jnp.where(positions == FAR_TILES - 1, CAP, counts).astype(jnp.int32)


def draw_far_offsets(key, part):
    slot_total = TILES_DEV * CAP

    def one_device(device):
        device_key = jax.random.fold_in(jax.random.fold_in(key, 7177), device)
        key_head, key_rest, key_order, key_local = jax.random.split(device_key, 4)
        head_owner = jax.random.randint(key_head, (), 0, N_COL)
        others = (head_owner + 1 + jax.random.permutation(key_rest, N_COL - 1)) % N_COL
        positions = jnp.arange(slot_total, dtype=jnp.int32)
        rest_index = jnp.maximum(positions - MOST, 0) % (N_COL - 1)
        owners = jnp.where(positions < MOST, head_owner, others[rest_index])
        owners = owners[jax.random.permutation(key_order, slot_total)]
        local_ids = jax.random.randint(key_local, (slot_total,), 0, RESP_DEV)
        return owners * RESP_DEV + local_ids
    offsets = jax.vmap(one_device)(jnp.arange(DEVICES, dtype=jnp.int32))
    return offsets.reshape(FAR_TILES, CAP).astype(jnp.int32)


def draw_near_cache(key, part):
    key_noise, key_rows, key_cols = jax.random.split(jax.random.fold_in(key, 4099), 3)
    magnitude = (TILE * FAR_TILES * CAP) ** (-0.5)
    random_part = jnp.clip(jax.random.normal(key_noise, (NNEAR, TILE, TILE), jnp.float32), -4.0, 4.0)
    row_factor = jnp.clip(jax.random.normal(key_rows, (TILE,), jnp.float32), -3.0, 3.0)
    col_factor = jnp.clip(jax.random.normal(key_cols, (TILE,), jnp.float32), -3.0, 3.0)
    strength = 3.6
    shared_part = strength / TILE ** 0.5 * row_factor[:, None] * col_factor[None, :]
    return (magnitude * (random_part + shared_part[None, :, :])).astype(jnp.bfloat16)


def place_ends(result, rng, smallest, high):
    longest = result.shape.index(max(result.shape))
    spots = []
    for shift in (0, 1):
        where = [jax.random.randint(jax.random.fold_in(rng, axis), (), 0, length) for axis, length in enumerate(result.shape)]
        where[longest] = (where[longest] + shift) % result.shape[longest]
        spots.append(tuple(where))
    return result.at[spots[0]].set(smallest).at[spots[1]].set(high)


def levels(own_key, extent, shards, low, largest):
    def one(dim, shards_of):
        heights = jax.random.uniform(jax.random.fold_in(jax.random.fold_in(own_key, 6), dim), (shards_of,), jnp.float32, low / len(shards), largest / len(shards))
        return jnp.repeat(jnp.exp(heights), extent[dim] // shards_of).reshape((-1,) + (1,) * (len(extent) - dim - 1))

    factor_of = one(*shards[0])
    for cut in shards[1:]:
        factor_of = factor_of * one(*cut)
    return factor_of


def centred(own_key, dims, spread, bound, shards=(), kind=jnp.bfloat16):
    array = spread * jax.random.normal(own_key, dims, jnp.float32)
    if shards:
        array = array * levels(own_key, dims, shards, -0.22, 0.18)
    return jnp.clip(array, -bound, bound).astype(kind)


def setup_inputs(seed: int = 0) -> dict:
    splits = jax.random.split(jax.random.key(seed), 8)
    return {
        "response_cache": centred(splits[0], (NRESP, TILE, TILE), (FAR_TILES ** 0.5), 128.0, ((0, 16),)),
        "near_cache": draw_near_cache(jax.random.fold_in(splits[7], 71), 0),
        "lead_diag": jnp.clip(jnp.exp(jax.random.uniform(splits[2], (2 * TILE,), jnp.float32, math.log(0.25), math.log(2.0))), 0.25, 2.0),
        "far_offsets": draw_far_offsets(jax.random.fold_in(splits[7], 71), 0),
        "near_first": place_ends(jax.random.randint(splits[4], (FAR_TILES, CAP), 0, NNEAR), jax.random.fold_in(splits[4], 1), 0, NNEAR - 1).astype(jnp.int32),
        "near_second": place_ends(jax.random.randint(splits[5], (FAR_TILES, CAP), 0, NNEAR), jax.random.fold_in(splits[5], 1), 0, NNEAR - 1).astype(jnp.int32),
        "tile_counts": draw_tile_counts(jax.random.fold_in(splits[7], 71), 0),
    }


def pair_table(near_first, near_second, usable, near_total):
    labels = jnp.arange(near_total, dtype=jnp.int32)
    first_hot = (near_first[:, :, None] == labels[None, None, :]).astype(jnp.float32) * usable[:, :, None]
    second_hot = (near_second[:, :, None] == labels[None, None, :]).astype(jnp.float32)
    return jnp.einsum('fsj,fsk->jk', first_hot, second_hot, precision=lax.Precision.HIGHEST)

def lead_gram(near_cache, pairs):
    near_total = near_cache.shape[0]
    tile_size = near_cache.shape[1]
    wide_near = jnp.transpose(near_cache, (1, 0, 2)).reshape(tile_size, near_total * tile_size)
    rows_first = jnp.sum(pairs, axis=1)
    rows_second = jnp.sum(pairs, axis=0)
    upper = jnp.zeros((tile_size, tile_size), jnp.float32)
    lower = jnp.zeros((tile_size, tile_size), jnp.float32)
    across = jnp.zeros((tile_size, tile_size), jnp.float32)
    for near_index in range(near_total):
        products = jnp.dot(near_cache[near_index].T.astype(jnp.float32), wide_near.astype(jnp.float32), preferred_element_type=jnp.float32)
        products = products.reshape(tile_size, near_total, tile_size)
        diagonal_part = products[:, near_index, :]
        upper = upper + rows_first[near_index] * diagonal_part
        lower = lower + rows_second[near_index] * diagonal_part
        across = across + jnp.einsum('akb,k->ab', products, pairs[:, near_index], precision=lax.Precision.HIGHEST)
    top_rows = jnp.concatenate([upper, across.T], axis=1)
    bottom_rows = jnp.concatenate([across, lower], axis=1)
    return jnp.concatenate([top_rows, bottom_rows], axis=0)

def factor_panels(hess_lead, far_hess, tile_size):
    first = jnp.linalg.cholesky(hess_lead[:tile_size, :tile_size])
    coupling = jax.scipy.linalg.solve_triangular(first, hess_lead[tile_size:, :tile_size].T, lower=True).T
    schur = hess_lead[tile_size:, tile_size:] - jnp.dot(coupling, coupling.T, precision=lax.Precision.HIGHEST)
    second = jnp.linalg.cholesky(schur)
    zero_block = jnp.zeros((tile_size, tile_size), jnp.float32)
    lead_factor = jnp.concatenate([jnp.concatenate([first, zero_block], axis=1), jnp.concatenate([coupling, second], axis=1)], axis=0)
    far_first = jax.scipy.linalg.solve_triangular(first, far_hess[:, :tile_size].T, lower=True).T
    updated = far_hess[:, tile_size:] - jnp.dot(far_first, coupling.T, precision=lax.Precision.HIGHEST)
    far_second = jax.scipy.linalg.solve_triangular(second, updated.T, lower=True).T
    return (lead_factor, jnp.concatenate([far_first, far_second], axis=1))

def reference(response_cache, near_cache, lead_diag, far_offsets, near_first, near_second, tile_counts):
    slot_ids = jnp.arange(CAP, dtype=jnp.int32)
    usable = (slot_ids[None, :] < tile_counts[:, None]).astype(jnp.float32)
    pairs = pair_table(near_first, near_second, usable, NNEAR)
    hess_lead = lead_gram(near_cache, pairs) + jnp.diag(lead_diag)

    def add_slot(slot_index, running):
        far_blocks = response_cache[far_offsets[:, slot_index]].astype(jnp.float32)
        near_blocks = jnp.concatenate([near_cache[near_first[:, slot_index]], near_cache[near_second[:, slot_index]]], axis=2).astype(jnp.float32)
        near_blocks = near_blocks * usable[:, slot_index][:, None, None]
        return running + jnp.einsum('tia,tib->tab', far_blocks, near_blocks, precision=lax.Precision.HIGHEST)
    far_hess = lax.fori_loop(0, CAP, add_slot, jnp.zeros((FAR_TILES, TILE, 2 * TILE), jnp.float32))
    far_hess = far_hess.reshape(FAR_TILES * TILE, 2 * TILE)
    return factor_panels(hess_lead, far_hess, TILE)
```

```python
import functools

import jax
import jax.numpy as jnp
from jax import lax
from jax.experimental import pallas as pl
from jax.experimental.pallas import tpu as pltpu
from jax.sharding import PartitionSpec as P

HIGHEST = lax.Precision.HIGHEST
BLOCK = 128
GROUP = 4


def dot32(left, right):
    return jnp.dot(left, right, precision=HIGHEST, preferred_element_type=jnp.float32)


def spread_rows(value, row):
    return jnp.broadcast_to(value[row : row + 1, :], (8, BLOCK))


def factor_block(block):
    groups = BLOCK // 8
    sub = lax.broadcasted_iota(jnp.int32, (8, BLOCK), 0)
    lane = lax.broadcasted_iota(jnp.int32, (8, BLOCK), 1)
    main = [block[8 * g : 8 * g + 8, :] for g in range(groups)]
    side = [(lane == sub + 8 * g).astype(jnp.float32) for g in range(groups)]
    for panel in range(groups):
        start = 8 * panel
        cols = {
            (g, m): jnp.broadcast_to(main[g][:, start + m : start + m + 1], (8, BLOCK))
            for g in range(panel, groups)
            for m in range(8)
        }
        scale = jnp.ones((8, BLOCK), jnp.float32)
        for j in range(8):
            pivots = {m: spread_rows(cols[panel, m], j) for m in range(j, 8)}
            root = lax.rsqrt(pivots[j])
            root = root * (1.5 - 0.5 * pivots[j] * root * root)
            inverse = root * root
            scale = jnp.where(sub == j, root, scale)
            main_row = spread_rows(main[panel], j)
            side_row = spread_rows(side[panel], j)
            for g in range(panel, groups):
                ratio = cols[g, j] * inverse
                if g == panel:
                    ratio = jnp.where(sub > j, ratio, 0.0)
                for m in range(j + 1, 8):
                    cols[g, m] = cols[g, m] - ratio * pivots[m]
                main[g] = main[g] - ratio * main_row
                side[g] = side[g] - ratio * side_row
        main[panel] = main[panel] * scale
        side[panel] = side[panel] * scale
    for g in range(groups):
        main[g] = jnp.where(lane >= sub + 8 * g, main[g], 0.0)
        side[g] = jnp.where(lane <= sub + 8 * g, side[g], 0.0)
    return jnp.concatenate(main, axis=0), jnp.concatenate(side, axis=0)


def lead_kernel(pairs_ref, near_ref, turned_ref, diag_ref, factor_ref, inverse_ref, work, upper):
    near_total, size, _ = near_ref.shape
    whole = 2 * size
    first_sums = [sum(pairs_ref[j, k] for k in range(near_total)) for j in range(near_total)]
    second_sums = [sum(pairs_ref[j, k] for j in range(near_total)) for k in range(near_total)]
    work[...] = jnp.zeros_like(work)
    for j in range(near_total):
        left = turned_ref[j]
        mixed = jnp.zeros((size, size), jnp.float32)
        for k in range(near_total):
            product = jnp.dot(left, near_ref[k], preferred_element_type=jnp.float32)
            mixed = mixed + pairs_ref[j, k] * product
            if k == j:
                own = product
        work[:size, :size] += first_sums[j] * own
        work[size:, size:whole] += second_sums[j] * own
        work[:size, size:whole] += mixed
    rows = lax.broadcasted_iota(jnp.int32, (whole, whole), 0)
    columns = lax.broadcasted_iota(jnp.int32, (whole, whole), 1)
    same = rows == columns
    work[:, :whole] += jnp.where(same, jnp.broadcast_to(diag_ref[...], (whole, whole)), 0.0)
    work[:, whole:] = same.astype(jnp.float32)

    def step(b, carry):
        base = pl.multiple_of(b * BLOCK, BLOCK)
        own = pl.ds(base, BLOCK)
        _, turned = factor_block(work[own, own])
        solved = dot32(turned, work[own, :])
        at = columns[:BLOCK, :] >= base + rows[:BLOCK, :]
        solved_main = jnp.where(at, solved[:, :whole], 0.0)
        upper[own, :] = solved_main
        work[own, whole:] = solved[:, whole:]
        below = jnp.where(columns[:BLOCK, :] >= base + BLOCK, solved_main, 0.0)
        change = dot32(below.T, jnp.concatenate([below, solved[:, whole:]], axis=1))
        work[...] = work[...] - change
        return carry

    lax.fori_loop(0, whole // BLOCK, step, 0)
    factor_ref[...] = upper[...].T
    inverse_ref[...] = work[:, whole:].T


def lead(pairs, near_cache, turned_near, lead_diag):
    whole = lead_diag.shape[0]
    vmem = pl.BlockSpec(memory_space=pltpu.VMEM)
    return pl.pallas_call(
        lead_kernel,
        out_shape=(
            jax.ShapeDtypeStruct((whole, whole), jnp.float32),
            jax.ShapeDtypeStruct((whole, whole), jnp.float32),
        ),
        in_specs=[pl.BlockSpec(memory_space=pltpu.SMEM), vmem, vmem, vmem],
        out_specs=(vmem, vmem),
        scratch_shapes=[
            pltpu.VMEM((whole, 2 * whole), jnp.float32),
            pltpu.VMEM((whole, whole), jnp.float32),
        ],
        compiler_params=pltpu.CompilerParams(vmem_limit_bytes=40 << 20),
        name="lead",
    )(pairs, near_cache, turned_near, lead_diag.reshape(1, whole))


def far_kernel(
    counts_ref, offsets_ref, first_ref, second_ref, blocks_ref, turned_ref, inverse_ref, out_ref,
    held, total, arrived,
):
    tiles, slots = offsets_ref.shape
    size = turned_ref.shape[1]
    tile = pl.program_id(0)
    rounds = slots // GROUP
    empty = turned_ref.shape[0] - 1

    def fetch(t, s):
        return pltpu.make_async_copy(
            blocks_ref.at[offsets_ref[t, s]],
            held.at[t, pl.ds(pl.multiple_of(s * size, size), size), :],
            arrived.at[t, s],
        )

    def rounds_of(t):
        return (counts_ref[t] + GROUP - 1) // GROUP

    @pl.when(tile == 0)
    def start():
        for t in range(tiles):
            def begin(s, carry):
                fetch(t, s).start()
                return carry

            lax.fori_loop(0, rounds_of(t) * GROUP, begin, 0)

    total[...] = jnp.zeros_like(total)

    def one_round(r, carry):
        for i in range(GROUP):
            fetch(tile, r * GROUP + i).wait()
        firsts = []
        seconds = []
        for i in range(GROUP):
            s = r * GROUP + i
            used = s < counts_ref[tile]
            firsts.append(turned_ref[jnp.where(used, first_ref[tile, s], empty)])
            seconds.append(turned_ref[jnp.where(used, second_ref[tile, s], empty)])
        left = jnp.concatenate(
            [jnp.concatenate(firsts, axis=1), jnp.concatenate(seconds, axis=1)], axis=0
        )
        span = GROUP * size
        right = held[tile, pl.ds(pl.multiple_of(r * span, span), span), :]
        total[...] += jnp.dot(left, right, preferred_element_type=jnp.float32)
        return carry

    lax.fori_loop(0, rounds_of(tile), one_round, 0)
    turned = total[...].T
    out_ref[:, :size] = dot32(turned[:, :size], inverse_ref[:size, :size])
    out_ref[:, size:] = dot32(turned, inverse_ref[:, size:])


def far(counts, offsets, near_first, near_second, blocks, turned_near, inverse):
    tiles, slots = offsets.shape
    size = blocks.shape[1]
    whole = lambda *shape: pl.BlockSpec(shape, lambda t, *_: (0,) * len(shape))
    return pl.pallas_call(
        far_kernel,
        out_shape=jax.ShapeDtypeStruct((tiles * size, 2 * size), jnp.float32),
        grid_spec=pltpu.PrefetchScalarGridSpec(
            num_scalar_prefetch=4,
            grid=(tiles,),
            in_specs=[
                pl.BlockSpec(memory_space=pl.ANY),
                whole(*turned_near.shape),
                whole(*inverse.shape),
            ],
            out_specs=pl.BlockSpec((size, 2 * size), lambda t, *_: (t, 0)),
            scratch_shapes=[
                pltpu.VMEM((tiles, slots * size, size), jnp.bfloat16),
                pltpu.VMEM((2 * size, size), jnp.float32),
                pltpu.SemaphoreType.DMA((tiles, slots)),
            ],
        ),
        compiler_params=pltpu.CompilerParams(
            dimension_semantics=("arbitrary",), vmem_limit_bytes=40 << 20
        ),
        name="far",
    )(counts, offsets, near_first, near_second, blocks, turned_near, inverse)


def local_pairs(near_first, near_second, counts, near_total):
    slots = near_first.shape[1]
    usable = jnp.arange(slots, dtype=jnp.int32)[None, :] < counts[:, None]
    labels = jnp.arange(near_total, dtype=jnp.int32)
    first_hot = (near_first[:, :, None] == labels) & usable[:, :, None]
    second_hot = near_second[:, :, None] == labels
    both = first_hot[:, :, :, None] & second_hot[:, :, None, :]
    return jnp.sum(both.astype(jnp.float32), axis=(0, 1))


def total_pairs(value):
    for axis, bits in (("row", (1, 4, 2)), ("col", (8, 4, 2, 1))):
        size = lax.axis_size(axis)
        for bit in bits:
            value = value + lax.ppermute(value, axis, [(i, i ^ bit) for i in range(size)])
    return value


def shards(
    response_cache, near_cache, lead_diag, far_offsets, near_first, near_second, tile_counts
):
    near_total = near_cache.shape[0]
    share = response_cache.shape[0] // lax.axis_size("row")
    own = lax.dynamic_slice_in_dim(response_cache, lax.axis_index("row") * share, share, 0)
    blocks = lax.all_gather(own, ("col", "row"), axis=0, tiled=True)
    pairs = total_pairs(local_pairs(near_first, near_second, tile_counts, near_total))
    turned = jnp.transpose(near_cache, (0, 2, 1))
    padded = jnp.concatenate([turned, jnp.zeros_like(turned[:1])], axis=0)
    lead_factor, inverse = lead(pairs, near_cache, turned, lead_diag)
    far_factor = far(
        tile_counts, far_offsets, near_first, near_second, blocks, padded, inverse
    )
    return lead_factor, far_factor


def solution(mesh):
    return jax.shard_map(
        shards,
        mesh=mesh,
        in_specs=(
            P("col", None, None),
            P(),
            P(),
            P(("row", "col"), None),
            P(("row", "col"), None),
            P(("row", "col"), None),
            P(("row", "col")),
        ),
        out_specs=(P(), P(("row", "col"), None)),
        check_vma=False,
    )
```

```python
import functools

import jax
import jax.numpy as jnp
from jax import lax
from jax.experimental import pallas as pl
from jax.experimental.pallas import tpu as pltpu
from jax.sharding import PartitionSpec as P

HIGHEST = lax.Precision.HIGHEST
BLOCK = 128
GROUP = 4
SIDE = 4
CACHED = 16
HALF = CACHED // 2
RING = 2


def dot32(left, right):
    return jnp.dot(left, right, precision=HIGHEST, preferred_element_type=jnp.float32)


def spread_rows(value, row):
    return jnp.broadcast_to(value[row : row + 1, :], (8, BLOCK))


def factor_block(block):
    groups = BLOCK // 8
    sub = lax.broadcasted_iota(jnp.int32, (8, BLOCK), 0)
    lane = lax.broadcasted_iota(jnp.int32, (8, BLOCK), 1)
    main = [block[8 * g : 8 * g + 8, :] for g in range(groups)]
    side = [(lane == sub + 8 * g).astype(jnp.float32) for g in range(groups)]
    for panel in range(groups):
        start = 8 * panel
        cols = {
            (g, m): jnp.broadcast_to(main[g][:, start + m : start + m + 1], (8, BLOCK))
            for g in range(panel, groups)
            for m in range(8)
        }
        scale = jnp.ones((8, BLOCK), jnp.float32)
        for j in range(8):
            pivots = {m: spread_rows(cols[panel, m], j) for m in range(j, 8)}
            root = lax.rsqrt(pivots[j])
            root = root * (1.5 - 0.5 * pivots[j] * root * root)
            inverse = root * root
            scale = jnp.where(sub == j, root, scale)
            main_row = spread_rows(main[panel], j)
            side_row = spread_rows(side[panel], j)
            for g in range(panel, groups):
                ratio = cols[g, j] * inverse
                if g == panel:
                    ratio = jnp.where(sub > j, ratio, 0.0)
                for m in range(j + 1, 8):
                    cols[g, m] = cols[g, m] - ratio * pivots[m]
                main[g] = main[g] - ratio * main_row
                side[g] = side[g] - ratio * side_row
        main[panel] = main[panel] * scale
        side[panel] = side[panel] * scale
    for g in range(groups):
        main[g] = jnp.where(lane >= sub + 8 * g, main[g], 0.0)
        side[g] = jnp.where(lane <= sub + 8 * g, side[g], 0.0)
    return jnp.concatenate(main, axis=0), jnp.concatenate(side, axis=0)


def factor_steps(work, upper, begin, end):
    whole = upper.shape[0]
    rows = lax.broadcasted_iota(jnp.int32, (BLOCK, whole), 0)
    columns = lax.broadcasted_iota(jnp.int32, (BLOCK, whole), 1)

    def step(b, carry):
        base = pl.multiple_of(b * BLOCK, BLOCK)
        own = pl.ds(base, BLOCK)
        _, turned = factor_block(work[own, own])
        solved = dot32(turned, work[own, :])
        solved_main = jnp.where(columns >= base + rows, solved[:, :whole], 0.0)
        upper[own, :] = solved_main
        work[own, whole:] = solved[:, whole:]
        below = jnp.where(columns >= base + BLOCK, solved_main, 0.0)
        change = dot32(below.T, jnp.concatenate([below, solved[:, whole:]], axis=1))
        work[...] = work[...] - change
        return carry

    lax.fori_loop(begin, end, step, 0)


def lead_start_kernel(pairs_ref, near_ref, turned_ref, diag_ref, work, upper):
    near_total, size, _ = near_ref.shape
    whole = 2 * size
    first_sums = [sum(pairs_ref[j, k] for k in range(near_total)) for j in range(near_total)]
    second_sums = [sum(pairs_ref[j, k] for j in range(near_total)) for k in range(near_total)]
    work[...] = jnp.zeros_like(work)
    for j in range(near_total):
        left = turned_ref[j]
        mixed = jnp.zeros((size, size), jnp.float32)
        for k in range(near_total):
            product = jnp.dot(left, near_ref[k], preferred_element_type=jnp.float32)
            mixed = mixed + pairs_ref[j, k] * product
            if k == j:
                own = product
        work[:size, :size] += first_sums[j] * own
        work[size:, size:whole] += second_sums[j] * own
        work[:size, size:whole] += mixed
    rows = lax.broadcasted_iota(jnp.int32, (whole, whole), 0)
    columns = lax.broadcasted_iota(jnp.int32, (whole, whole), 1)
    same = rows == columns
    work[:, :whole] += jnp.where(same, jnp.broadcast_to(diag_ref[...], (whole, whole)), 0.0)
    work[:, whole:] = same.astype(jnp.float32)
    factor_steps(work, upper, 0, size // BLOCK)


def lead_end_kernel(work_ref, upper_ref, factor_ref, inverse_ref, work, upper):
    whole = upper.shape[0]
    half = whole // 2
    work[...] = work_ref[...]
    upper[:half, :] = upper_ref[:half, :]
    factor_steps(work, upper, half // BLOCK, whole // BLOCK)
    factor_ref[...] = upper[...].T
    inverse_ref[...] = work[:, whole:].T


VMEM = pl.BlockSpec(memory_space=pltpu.VMEM)


def lead_start(pairs, near_cache, turned_near, lead_diag):
    whole = lead_diag.shape[0]
    return pl.pallas_call(
        lead_start_kernel,
        out_shape=(
            jax.ShapeDtypeStruct((whole, 2 * whole), jnp.float32),
            jax.ShapeDtypeStruct((whole, whole), jnp.float32),
        ),
        in_specs=[pl.BlockSpec(memory_space=pltpu.SMEM), VMEM, VMEM, VMEM],
        out_specs=(VMEM, VMEM),
        compiler_params=pltpu.CompilerParams(vmem_limit_bytes=24 << 20),
        cost_estimate=pl.CostEstimate(
            flops=9_000_000_000, bytes_accessed=6 << 20, transcendentals=0
        ),
        name="lead_start",
    )(pairs, near_cache, turned_near, lead_diag.reshape(1, whole))


def lead_end(work, upper):
    whole = upper.shape[0]
    square = jax.ShapeDtypeStruct((whole, whole), jnp.float32)
    return pl.pallas_call(
        lead_end_kernel,
        out_shape=(square, square),
        in_specs=[VMEM, VMEM],
        out_specs=(VMEM, VMEM),
        scratch_shapes=[
            pltpu.VMEM((whole, 2 * whole), jnp.float32),
            pltpu.VMEM((whole, whole), jnp.float32),
        ],
        compiler_params=pltpu.CompilerParams(vmem_limit_bytes=24 << 20),
        cost_estimate=pl.CostEstimate(
            flops=9_000_000_000, bytes_accessed=6 << 20, transcendentals=0
        ),
        name="lead_end",
    )(work, upper)


def position():
    row, col = lax.axis_index("row"), lax.axis_index("col")
    return row % 2, col // SIDE, col % SIDE


def ring_slot(offset, here):
    core, y, z = here
    col, local = offset // CACHED, offset % CACHED
    half, inner = local // HALF, local % HALF
    sign = 1 - 2 * core
    from_y = (sign * (y - col // SIDE)) & (SIDE - 1)
    from_z = (sign * (z - col % SIDE)) & (SIDE - 1)
    by_z = inner < RING
    major = jnp.where(by_z, from_z, from_y)
    minor = jnp.where(by_z, from_y, from_z)
    place = jnp.where(by_z, inner, inner - RING + SIDE * SIDE * RING)
    held = (half == core) & (inner < 2 * RING)
    return held, (major * SIDE + minor) * RING + place


def spread_slot(offset):
    col, local = offset // CACHED, offset % CACHED
    half, inner = local // HALF, local % HALF
    kept = HALF - 2 * RING
    return inner >= 2 * RING, col * (2 * kept) + half * kept + inner - 2 * RING


def list_slots(tile, slot_of, info_ref, items, slots):
    def visit(s, count):
        wanted, place = slot_of(info_ref[tile, s])
        items[0, tile, count] = place
        items[1, tile, count] = info_ref[tile, slots + s]
        items[2, tile, count] = info_ref[tile, 2 * slots + s]
        wanted = wanted & (s < info_ref[tile, 3 * slots])
        return count + wanted.astype(jnp.int32)

    return lax.fori_loop(0, slots, visit, 0)


def left_rows(tile, r, count, items, turned_ref):
    empty = turned_ref.shape[0] - 1
    firsts, seconds = [], []
    for i in range(GROUP):
        q = r * GROUP + i
        used = q < count
        firsts.append(turned_ref[jnp.where(used, items[1, tile, q], empty)])
        seconds.append(turned_ref[jnp.where(used, items[2, tile, q], empty)])
    return jnp.concatenate(
        [jnp.concatenate(firsts, axis=1), jnp.concatenate(seconds, axis=1)], axis=0
    )


def ring_kernel(slots, seeded, info_ref, *refs):
    if seeded:
        seed_ref, turned_ref = refs[:2]
        refs = refs[2:]
    else:
        turned_ref = refs[0]
        refs = refs[1:]
    *pieces, out_ref, held, items, arrived = refs
    size = turned_ref.shape[1]
    tile = pl.program_id(0)
    here = position()
    copies = []
    start = 0
    for n, piece in enumerate(pieces):
        copies.append(
            pltpu.make_async_copy(piece, held.at[pl.ds(start, piece.shape[0])], arrived.at[n])
        )
        start += piece.shape[0]

    @pl.when(tile == 0)
    def fetch():
        for copy in copies:
            copy.start()

    count = list_slots(tile, lambda offset: ring_slot(offset, here), info_ref, items, slots)

    @pl.when(tile == 0)
    def wait():
        for copy in copies:
            copy.wait()

    out_ref[...] = seed_ref[...] if seeded else jnp.zeros_like(out_ref)

    def one_round(r, carry):
        rights = []
        for i in range(GROUP):
            q = r * GROUP + i
            rights.append(held[jnp.where(q < count, items[0, tile, q], 0)])
        out_ref[0] += jnp.dot(
            left_rows(tile, r, count, items, turned_ref),
            jnp.concatenate(rights, axis=0),
            preferred_element_type=jnp.float32,
        )
        return carry

    lax.fori_loop(0, (count + GROUP - 1) // GROUP, one_round, 0)


def ring_sums(info, slots, turned_near, pieces, seed=None):
    tiles = info.shape[0]
    size = turned_near.shape[1]
    per_tile = pl.BlockSpec((1, 2 * size, size), lambda t, *_: (t, 0, 0))
    seeds = [] if seed is None else [seed]
    return pl.pallas_call(
        functools.partial(ring_kernel, slots, seed is not None),
        out_shape=jax.ShapeDtypeStruct((tiles, 2 * size, size), jnp.float32),
        grid_spec=pltpu.PrefetchScalarGridSpec(
            num_scalar_prefetch=1,
            grid=(tiles,),
            in_specs=[per_tile] * len(seeds)
            + [pl.BlockSpec(turned_near.shape, lambda t, *_: (0, 0, 0))]
            + [pl.BlockSpec(memory_space=pltpu.HBM)] * len(pieces),
            out_specs=per_tile,
            scratch_shapes=[
                pltpu.VMEM((sum(p.shape[0] for p in pieces), size, size), jnp.bfloat16),
                pltpu.SMEM((3, tiles, slots), jnp.int32),
                pltpu.SemaphoreType.DMA((len(pieces),)),
            ],
        ),
        compiler_params=pltpu.CompilerParams(
            dimension_semantics=("arbitrary",), vmem_limit_bytes=60 << 20
        ),
        cost_estimate=pl.CostEstimate(
            flops=3_000_000_000, bytes_accessed=12 << 20, transcendentals=0
        ),
        name="ring_sums",
    )(info, *seeds, turned_near, *pieces)


def far_kernel(
    slots, info_ref, sums_ref, blocks_ref, turned_hbm, inverse_hbm, out_hbm, held, total,
    turned_ref, inverse_ref, out_ref, items, arrived, loaded, stored,
):
    tiles = info_ref.shape[0]
    size = turned_ref.shape[1]
    span = GROUP * size

    def fetch(t, q, place):
        return pltpu.make_async_copy(
            blocks_ref.at[place],
            held.at[t, pl.ds(pl.multiple_of(q * size, size), size), :],
            arrived.at[t, q],
        )

    def store(t):
        return pltpu.make_async_copy(
            out_ref.at[t], out_hbm.at[pl.ds(t * size, size), :], stored.at[t]
        )

    load_turned = pltpu.make_async_copy(turned_hbm, turned_ref, loaded.at[0])
    load_sums = pltpu.make_async_copy(sums_ref, total, loaded.at[1])
    load_inverse = pltpu.make_async_copy(inverse_hbm, inverse_ref, loaded.at[2])
    load_turned.start()
    load_sums.start()
    counts = []
    for t in range(tiles):
        count = list_slots(t, spread_slot, info_ref, items, slots)
        counts.append(count)

        def begin(q, carry):
            fetch(t, q, jnp.where(q < count, items[0, t, q], 0)).start()
            return carry

        lax.fori_loop(0, (count + GROUP - 1) // GROUP * GROUP, begin, 0)
    load_inverse.start()
    load_turned.wait()
    load_sums.wait()
    for t in range(tiles):

        def one_round(r, carry):
            for i in range(GROUP):
                fetch(t, r * GROUP + i, 0).wait()
            right = held[t, pl.ds(pl.multiple_of(r * span, span), span), :]
            total[t] += jnp.dot(
                left_rows(t, r, counts[t], items, turned_ref),
                right,
                preferred_element_type=jnp.float32,
            )
            return carry

        lax.fori_loop(0, (counts[t] + GROUP - 1) // GROUP, one_round, 0)
        if t == 0:
            load_inverse.wait()
        turned = total[t].T
        out_ref[t, :, :size] = dot32(turned[:, :size], inverse_ref[:size, :size])
        out_ref[t, :, size:] = dot32(turned, inverse_ref[:, size:])
        store(t).start()
    for t in range(tiles):
        store(t).wait()


HBM = pl.BlockSpec(memory_space=pltpu.HBM)


def far(info, slots, sums, blocks, turned_near, inverse):
    tiles = info.shape[0]
    size = blocks.shape[1]
    return pl.pallas_call(
        functools.partial(far_kernel, slots),
        out_shape=jax.ShapeDtypeStruct((tiles * size, 2 * size), jnp.float32),
        in_specs=[pl.BlockSpec(memory_space=pltpu.SMEM), HBM, HBM, HBM, HBM],
        out_specs=HBM,
        scratch_shapes=[
            pltpu.VMEM((tiles, slots * size, size), jnp.bfloat16),
            pltpu.VMEM(sums.shape, jnp.float32),
            pltpu.VMEM(turned_near.shape, jnp.bfloat16),
            pltpu.VMEM(inverse.shape, jnp.float32),
            pltpu.VMEM((tiles, size, 2 * size), jnp.float32),
            pltpu.SMEM((3, tiles, slots), jnp.int32),
            pltpu.SemaphoreType.DMA((tiles, slots)),
            pltpu.SemaphoreType.DMA((3,)),
            pltpu.SemaphoreType.DMA((tiles,)),
        ],
        compiler_params=pltpu.CompilerParams(vmem_limit_bytes=63 << 20),
        name="far",
    )(info, sums, blocks, turned_near, inverse)


def local_pairs(near_first, near_second, counts, near_total):
    slots = near_first.shape[1]
    usable = jnp.arange(slots, dtype=jnp.int32)[None, :] < counts[:, None]
    labels = jnp.arange(near_total, dtype=jnp.int32)
    first_hot = (near_first[:, :, None] == labels) & usable[:, :, None]
    second_hot = near_second[:, :, None] == labels
    both = first_hot[:, :, :, None] & second_hot[:, :, None, :]
    return jnp.sum(both.astype(jnp.float32), axis=(0, 1))


def hop(value, along_y):
    rows, cols = lax.axis_size("row"), lax.axis_size("col")
    moves = []
    for row in range(rows):
        sign = 1 - 2 * (row % 2)
        for col in range(cols):
            y, z = col // SIDE, col % SIDE
            y, z = ((y + sign) % SIDE, z) if along_y else (y, (z + sign) % SIDE)
            moves.append((row * cols + col, row * cols + y * SIDE + z))
    return lax.ppermute(value, ("row", "col"), moves)


def swap(value, axis, bit):
    return lax.ppermute(value, axis, [(i, i ^ bit) for i in range(lax.axis_size(axis))])


def shards(
    response_cache, near_cache, lead_diag, far_offsets, near_first, near_second, tile_counts
):
    near_total = near_cache.shape[0]
    slots = far_offsets.shape[1]
    row = lax.axis_index("row")
    core = row % 2
    kept = HALF - 2 * RING
    share = 2 * kept // lax.axis_size("row")
    at = row * share
    own = lax.dynamic_slice_in_dim(
        response_cache, at // kept * HALF + 2 * RING + at % kept, share, 0
    )
    blocks = lax.all_gather(own, ("col", "row"), axis=0, tiled=True)
    line_y = [lax.dynamic_slice_in_dim(response_cache, core * HALF, RING, 0)]
    line_z = [lax.dynamic_slice_in_dim(response_cache, core * HALF + RING, RING, 0)]
    pairs = local_pairs(near_first, near_second, tile_counts, near_total)
    for stages in (
        (("row", 1), ("row", 4), ("row", 2)),
        (("col", 8), ("col", 4)),
        (("col", 2), ("col", 1)),
    ):
        line_y.append(hop(line_y[-1], True))
        line_z.append(hop(line_z[-1], False))
        for axis, bit in stages:
            pairs = pairs + swap(pairs, axis, bit)
        pairs, line_y[-1], line_z[-1] = lax.optimization_barrier((pairs, line_y[-1], line_z[-1]))
    info = jnp.concatenate([far_offsets, near_first, near_second, tile_counts[:, None]], axis=1)
    info_other = swap(info, "row", 1)
    turned = jnp.transpose(near_cache, (0, 2, 1))
    padded = jnp.concatenate([turned, jnp.zeros_like(turned[:1])], axis=0)
    by_z = [jnp.concatenate(line_y, axis=0)]
    by_y = [jnp.concatenate(line_z, axis=0)]
    pairs, by_z[0], by_y[0] = lax.optimization_barrier((pairs, by_z[0], by_y[0]))
    by_z.append(hop(by_z[0], False))
    by_y.append(hop(by_y[0], True))
    work, upper = lead_start(pairs, near_cache, turned, lead_diag)
    work, by_z[1], by_y[1] = lax.optimization_barrier((work, by_z[1], by_y[1]))
    by_z.append(hop(by_z[1], False))
    by_y.append(hop(by_y[1], True))
    lead_factor, inverse = lead_end(work, upper)
    inverse, by_z[2], by_y[2] = lax.optimization_barrier((inverse, by_z[2], by_y[2]))
    by_z.append(hop(by_z[2], False))
    by_y.append(hop(by_y[2], True))
    pieces = by_z + by_y
    sums_other = swap(ring_sums(info_other, slots, padded, pieces), "row", 1)
    sums = ring_sums(info, slots, padded, pieces, sums_other)
    far_factor = far(info, slots, sums, blocks, padded, inverse)
    return lead_factor, far_factor


def solution(mesh):
    return jax.shard_map(
        shards,
        mesh=mesh,
        in_specs=(
            P("col", None, None),
            P(),
            P(),
            P(("row", "col"), None),
            P(("row", "col"), None),
            P(("row", "col"), None),
            P(("row", "col")),
        ),
        out_specs=(P(), P(("row", "col"), None)),
        check_vma=False,
    )
```

```python
import functools

import jax
import jax.numpy as jnp
from jax import lax
from jax.experimental import pallas as pl
from jax.experimental.pallas import tpu as pltpu
from jax.sharding import PartitionSpec as P

HIGHEST = lax.Precision.HIGHEST
BLOCK = 128
GROUP = 4
SIDE = 4
CACHED = 16
HALF = CACHED // 2
RING = 2


def dot32(left, right):
    return jnp.dot(left, right, precision=HIGHEST, preferred_element_type=jnp.float32)


def spread_rows(value, row):
    return jnp.broadcast_to(value[row : row + 1, :], (8, BLOCK))


def factor_block(block):
    groups = BLOCK // 8
    sub = lax.broadcasted_iota(jnp.int32, (8, BLOCK), 0)
    lane = lax.broadcasted_iota(jnp.int32, (8, BLOCK), 1)
    main = [block[8 * g : 8 * g + 8, :] for g in range(groups)]
    side = [(lane == sub + 8 * g).astype(jnp.float32) for g in range(groups)]
    for panel in range(groups):
        start = 8 * panel
        cols = {
            (g, m): jnp.broadcast_to(main[g][:, start + m : start + m + 1], (8, BLOCK))
            for g in range(panel, groups)
            for m in range(8)
        }
        scale = jnp.ones((8, BLOCK), jnp.float32)
        for j in range(8):
            pivots = {m: spread_rows(cols[panel, m], j) for m in range(j, 8)}
            root = lax.rsqrt(pivots[j])
            root = root * (1.5 - 0.5 * pivots[j] * root * root)
            inverse = root * root
            scale = jnp.where(sub == j, root, scale)
            main_row = spread_rows(main[panel], j)
            side_row = spread_rows(side[panel], j)
            for g in range(panel, groups):
                ratio = cols[g, j] * inverse
                if g == panel:
                    ratio = jnp.where(sub > j, ratio, 0.0)
                for m in range(j + 1, 8):
                    cols[g, m] = cols[g, m] - ratio * pivots[m]
                main[g] = main[g] - ratio * main_row
                side[g] = side[g] - ratio * side_row
        main[panel] = main[panel] * scale
        side[panel] = side[panel] * scale
    for g in range(groups):
        main[g] = jnp.where(lane >= sub + 8 * g, main[g], 0.0)
        side[g] = jnp.where(lane <= sub + 8 * g, side[g], 0.0)
    return jnp.concatenate(main, axis=0), jnp.concatenate(side, axis=0)


def factor_steps(work, upper, begin, end):
    whole = upper.shape[0]
    rows = lax.broadcasted_iota(jnp.int32, (BLOCK, whole), 0)
    columns = lax.broadcasted_iota(jnp.int32, (BLOCK, whole), 1)

    def step(b, carry):
        base = pl.multiple_of(b * BLOCK, BLOCK)
        own = pl.ds(base, BLOCK)
        _, turned = factor_block(work[own, own])
        solved = dot32(turned, work[own, :])
        solved_main = jnp.where(columns >= base + rows, solved[:, :whole], 0.0)
        upper[own, :] = solved_main
        work[own, whole:] = solved[:, whole:]
        below = jnp.where(columns >= base + BLOCK, solved_main, 0.0)
        change = dot32(below.T, jnp.concatenate([below, solved[:, whole:]], axis=1))
        work[...] = work[...] - change
        return carry

    lax.fori_loop(begin, end, step, 0)


def lead_start_kernel(pairs_ref, near_ref, turned_ref, diag_ref, work, upper):
    near_total, size, _ = near_ref.shape
    whole = 2 * size
    first_sums = [sum(pairs_ref[j, k] for k in range(near_total)) for j in range(near_total)]
    second_sums = [sum(pairs_ref[j, k] for j in range(near_total)) for k in range(near_total)]
    work[...] = jnp.zeros_like(work)
    for j in range(near_total):
        left = turned_ref[j]
        mixed = jnp.zeros((size, size), jnp.float32)
        for k in range(near_total):
            product = jnp.dot(left, near_ref[k], preferred_element_type=jnp.float32)
            mixed = mixed + pairs_ref[j, k] * product
            if k == j:
                own = product
        work[:size, :size] += first_sums[j] * own
        work[size:, size:whole] += second_sums[j] * own
        work[:size, size:whole] += mixed
    rows = lax.broadcasted_iota(jnp.int32, (whole, whole), 0)
    columns = lax.broadcasted_iota(jnp.int32, (whole, whole), 1)
    same = rows == columns
    work[:, :whole] += jnp.where(same, jnp.broadcast_to(diag_ref[...], (whole, whole)), 0.0)
    work[:, whole:] = same.astype(jnp.float32)
    factor_steps(work, upper, 0, size // BLOCK)


def lead_end_kernel(work_ref, upper_ref, factor_ref, inverse_ref, work, upper):
    whole = upper.shape[0]
    half = whole // 2
    work[...] = work_ref[...]
    upper[:half, :] = upper_ref[:half, :]
    factor_steps(work, upper, half // BLOCK, whole // BLOCK)
    factor_ref[...] = upper[...].T
    inverse_ref[...] = work[:, whole:].T


VMEM = pl.BlockSpec(memory_space=pltpu.VMEM)


def lead_start(pairs, near_cache, turned_near, lead_diag):
    whole = lead_diag.shape[0]
    return pl.pallas_call(
        lead_start_kernel,
        out_shape=(
            jax.ShapeDtypeStruct((whole, 2 * whole), jnp.float32),
            jax.ShapeDtypeStruct((whole, whole), jnp.float32),
        ),
        in_specs=[pl.BlockSpec(memory_space=pltpu.SMEM), VMEM, VMEM, VMEM],
        out_specs=(VMEM, VMEM),
        compiler_params=pltpu.CompilerParams(vmem_limit_bytes=24 << 20),
        cost_estimate=pl.CostEstimate(
            flops=9_000_000_000, bytes_accessed=6 << 20, transcendentals=0
        ),
        name="lead_start",
    )(pairs, near_cache, turned_near, lead_diag.reshape(1, whole))


def lead_end(work, upper):
    whole = upper.shape[0]
    square = jax.ShapeDtypeStruct((whole, whole), jnp.float32)
    return pl.pallas_call(
        lead_end_kernel,
        out_shape=(square, square),
        in_specs=[VMEM, VMEM],
        out_specs=(VMEM, VMEM),
        scratch_shapes=[
            pltpu.VMEM((whole, 2 * whole), jnp.float32),
            pltpu.VMEM((whole, whole), jnp.float32),
        ],
        compiler_params=pltpu.CompilerParams(vmem_limit_bytes=24 << 20),
        cost_estimate=pl.CostEstimate(
            flops=9_000_000_000, bytes_accessed=6 << 20, transcendentals=0
        ),
        name="lead_end",
    )(work, upper)


def ring_places(offsets, core, y, z):
    col, local = offsets // CACHED, offsets % CACHED
    half, inner = local // HALF, local % HALF
    sign = 1 - 2 * core
    from_y = (sign * (y - col // SIDE)) & (SIDE - 1)
    from_z = (sign * (z - col % SIDE)) & (SIDE - 1)
    by_z = inner < RING
    major = jnp.where(by_z, from_z, from_y)
    minor = jnp.where(by_z, from_y, from_z)
    place = jnp.where(by_z, inner, inner - RING + SIDE * SIDE * RING)
    held = (half == core) & (inner < 2 * RING)
    return jnp.where(held, (major * SIDE + minor) * RING + place, -1)


def spread_places(offsets):
    col, local = offsets // CACHED, offsets % CACHED
    half, inner = local // HALF, local % HALF
    kept = HALF - 2 * RING
    place = col * (2 * kept) + half * kept + inner - 2 * RING
    return jnp.where(inner >= 2 * RING, place, -1)


def list_slots(tile, info_ref, items, slots):
    def visit(s, count):
        place = info_ref[tile, s]
        items[0, tile, count] = place
        items[1, tile, count] = info_ref[tile, slots + s]
        items[2, tile, count] = info_ref[tile, 2 * slots + s]
        return count + (place >= 0).astype(jnp.int32)

    return lax.fori_loop(0, slots, visit, 0)


def left_rows(tile, r, count, items, turned_ref):
    empty = turned_ref.shape[0] - 1
    firsts, seconds = [], []
    for i in range(GROUP):
        q = r * GROUP + i
        used = q < count
        firsts.append(turned_ref[jnp.where(used, items[1, tile, q], empty)])
        seconds.append(turned_ref[jnp.where(used, items[2, tile, q], empty)])
    return jnp.concatenate(
        [jnp.concatenate(firsts, axis=1), jnp.concatenate(seconds, axis=1)], axis=0
    )


def ring_kernel(slots, info_ref, turned_ref, *refs):
    *pieces, out_ref, held, items, arrived = refs
    size = turned_ref.shape[1]
    tile = pl.program_id(0)
    copies = []
    start = 0
    for n, piece in enumerate(pieces):
        copies.append(
            pltpu.make_async_copy(piece, held.at[pl.ds(start, piece.shape[0])], arrived.at[n])
        )
        start += piece.shape[0]

    @pl.when(tile == 0)
    def fetch():
        for copy in copies:
            copy.start()

    count = list_slots(tile, info_ref, items, slots)

    @pl.when(tile == 0)
    def wait():
        for copy in copies:
            copy.wait()

    out_ref[...] = jnp.zeros_like(out_ref)

    def one_round(r, carry):
        rights = []
        for i in range(GROUP):
            q = r * GROUP + i
            rights.append(held[jnp.where(q < count, items[0, tile, q], 0)])
        out_ref[0] += jnp.dot(
            left_rows(tile, r, count, items, turned_ref),
            jnp.concatenate(rights, axis=0),
            preferred_element_type=jnp.float32,
        )
        return carry

    lax.fori_loop(0, (count + GROUP - 1) // GROUP, one_round, 0)


def ring_sums(info, slots, turned_near, pieces):
    tiles = info.shape[0]
    size = turned_near.shape[1]
    per_tile = pl.BlockSpec((1, 2 * size, size), lambda t, *_: (t, 0, 0))
    return pl.pallas_call(
        functools.partial(ring_kernel, slots),
        out_shape=jax.ShapeDtypeStruct((tiles, 2 * size, size), jnp.float32),
        grid_spec=pltpu.PrefetchScalarGridSpec(
            num_scalar_prefetch=1,
            grid=(tiles,),
            in_specs=[pl.BlockSpec(turned_near.shape, lambda t, *_: (0, 0, 0))]
            + [pl.BlockSpec(memory_space=pltpu.HBM)] * len(pieces),
            out_specs=per_tile,
            scratch_shapes=[
                pltpu.VMEM((sum(p.shape[0] for p in pieces), size, size), jnp.bfloat16),
                pltpu.SMEM((3, tiles, slots), jnp.int32),
                pltpu.SemaphoreType.DMA((len(pieces),)),
            ],
        ),
        compiler_params=pltpu.CompilerParams(
            dimension_semantics=("arbitrary",), vmem_limit_bytes=60 << 20
        ),
        cost_estimate=pl.CostEstimate(
            flops=3_000_000_000, bytes_accessed=12 << 20, transcendentals=0
        ),
        name="ring_sums",
    )(info, turned_near, *pieces)


def far_kernel(
    slots, info_ref, own_hbm, other_hbm, blocks_ref, turned_hbm, inverse_hbm, out_hbm, held, total,
    other_ref, turned_ref, inverse_ref, out_ref, items, arrived, loaded, stored,
):
    tiles = info_ref.shape[0]
    size = turned_ref.shape[1]
    span = GROUP * size

    def fetch(t, q, place):
        return pltpu.make_async_copy(
            blocks_ref.at[place],
            held.at[t, pl.ds(pl.multiple_of(q * size, size), size), :],
            arrived.at[t, q],
        )

    def store(t):
        return pltpu.make_async_copy(
            out_ref.at[t], out_hbm.at[pl.ds(t * size, size), :], stored.at[t]
        )

    load_turned = pltpu.make_async_copy(turned_hbm, turned_ref, loaded.at[0])
    load_own = pltpu.make_async_copy(own_hbm, total, loaded.at[1])
    load_inverse = pltpu.make_async_copy(inverse_hbm, inverse_ref, loaded.at[2])
    load_other = pltpu.make_async_copy(other_hbm, other_ref, loaded.at[3])
    load_turned.start()
    load_own.start()
    counts = []
    for t in range(tiles):
        count = list_slots(t, info_ref, items, slots)
        counts.append(count)

        def begin(q, carry):
            fetch(t, q, jnp.where(q < count, items[0, t, q], 0)).start()
            return carry

        lax.fori_loop(0, (count + GROUP - 1) // GROUP * GROUP, begin, 0)
    load_other.start()
    load_inverse.start()
    load_turned.wait()
    load_own.wait()
    for t in range(tiles):

        def one_round(r, carry):
            for i in range(GROUP):
                fetch(t, r * GROUP + i, 0).wait()
            right = held[t, pl.ds(pl.multiple_of(r * span, span), span), :]
            total[t] += jnp.dot(
                left_rows(t, r, counts[t], items, turned_ref),
                right,
                preferred_element_type=jnp.float32,
            )
            return carry

        lax.fori_loop(0, (counts[t] + GROUP - 1) // GROUP, one_round, 0)
        if t == 0:
            load_other.wait()
            load_inverse.wait()
        turned = (total[t] + other_ref[t]).T
        out_ref[t, :, :size] = dot32(turned[:, :size], inverse_ref[:size, :size])
        out_ref[t, :, size:] = dot32(turned, inverse_ref[:, size:])
        store(t).start()
    for t in range(tiles):
        store(t).wait()


HBM = pl.BlockSpec(memory_space=pltpu.HBM)


def far(info, slots, sums, other_sums, blocks, turned_near, inverse):
    tiles = info.shape[0]
    size = blocks.shape[1]
    return pl.pallas_call(
        functools.partial(far_kernel, slots),
        out_shape=jax.ShapeDtypeStruct((tiles * size, 2 * size), jnp.float32),
        in_specs=[pl.BlockSpec(memory_space=pltpu.SMEM)] + [HBM] * 5,
        out_specs=HBM,
        scratch_shapes=[
            pltpu.VMEM((tiles, slots * size, size), jnp.bfloat16),
            pltpu.VMEM(sums.shape, jnp.float32),
            pltpu.VMEM(sums.shape, jnp.float32),
            pltpu.VMEM(turned_near.shape, jnp.bfloat16),
            pltpu.VMEM(inverse.shape, jnp.float32),
            pltpu.VMEM((tiles, size, 2 * size), jnp.float32),
            pltpu.SMEM((3, tiles, slots), jnp.int32),
            pltpu.SemaphoreType.DMA((tiles, slots)),
            pltpu.SemaphoreType.DMA((4,)),
            pltpu.SemaphoreType.DMA((tiles,)),
        ],
        compiler_params=pltpu.CompilerParams(vmem_limit_bytes=63 << 20),
        name="far",
    )(info, sums, other_sums, blocks, turned_near, inverse)


def local_pairs(near_first, near_second, counts, near_total):
    slots = near_first.shape[1]
    usable = jnp.arange(slots, dtype=jnp.int32)[None, :] < counts[:, None]
    labels = jnp.arange(near_total, dtype=jnp.int32)
    first_hot = (near_first[:, :, None] == labels) & usable[:, :, None]
    second_hot = near_second[:, :, None] == labels
    both = first_hot[:, :, :, None] & second_hot[:, :, None, :]
    return jnp.sum(both.astype(jnp.float32), axis=(0, 1))


def hop(value, along_y):
    rows, cols = lax.axis_size("row"), lax.axis_size("col")
    moves = []
    for row in range(rows):
        sign = 1 - 2 * (row % 2)
        for col in range(cols):
            y, z = col // SIDE, col % SIDE
            y, z = ((y + sign) % SIDE, z) if along_y else (y, (z + sign) % SIDE)
            moves.append((row * cols + col, row * cols + y * SIDE + z))
    return lax.ppermute(value, ("row", "col"), moves)


def swap(value, axis, bit):
    return lax.ppermute(value, axis, [(i, i ^ bit) for i in range(lax.axis_size(axis))])


def shards(
    response_cache, near_cache, lead_diag, far_offsets, near_first, near_second, tile_counts
):
    near_total = near_cache.shape[0]
    slots = far_offsets.shape[1]
    row = lax.axis_index("row")
    core = row % 2
    kept = HALF - 2 * RING
    share = 2 * kept // lax.axis_size("row")
    at = row * share
    own = lax.dynamic_slice_in_dim(
        response_cache, at // kept * HALF + 2 * RING + at % kept, share, 0
    )
    blocks = lax.all_gather(own, ("col", "row"), axis=0, tiled=True)
    line_y = [lax.dynamic_slice_in_dim(response_cache, core * HALF, RING, 0)]
    line_z = [lax.dynamic_slice_in_dim(response_cache, core * HALF + RING, RING, 0)]
    usable = jnp.arange(slots, dtype=jnp.int32)[None, :] < tile_counts[:, None]
    y, z = lax.axis_index("col") // SIDE, lax.axis_index("col") % SIDE
    info, info_own, info_other = (
        jnp.concatenate([jnp.where(usable, places, -1), near_first, near_second], axis=1)
        for places in (
            spread_places(far_offsets),
            ring_places(far_offsets, core, y, z),
            ring_places(far_offsets, 1 - core, y, z),
        )
    )
    turned = jnp.transpose(near_cache, (0, 2, 1))
    padded = jnp.concatenate([turned, jnp.zeros_like(turned[:1])], axis=0)
    pairs = local_pairs(near_first, near_second, tile_counts, near_total)

    def advance(pairs, rings, stages):
        (to_z, along_y), (to_y, along_z) = rings
        to_z, to_y = hop(to_z, along_y), hop(to_y, along_z)
        for axis, bit in stages:
            pairs = pairs + swap(pairs, axis, bit)
        return lax.optimization_barrier((pairs, to_z, to_y))

    for stages in ((("row", 1),), (("row", 4),), (("row", 2),)):
        pairs, step_y, step_z = advance(
            pairs, ((line_y[-1], True), (line_z[-1], False)), stages
        )
        line_y.append(step_y)
        line_z.append(step_z)
    by_z = [jnp.concatenate(line_y, axis=0)]
    by_y = [jnp.concatenate(line_z, axis=0)]
    pairs, step_z, step_y = advance(
        pairs, ((by_z[-1], False), (by_y[-1], True)), (("col", 8), ("col", 4), ("col", 2))
    )
    by_z.append(step_z)
    by_y.append(step_y)
    info_other = swap(info_other, "row", 1)
    pairs = pairs + swap(pairs, "col", 1)
    step_z, step_y = hop(by_z[-1], False), hop(by_y[-1], True)
    work, upper = lead_start(pairs, near_cache, turned, lead_diag)
    work, step_z, step_y = lax.optimization_barrier((work, step_z, step_y))
    by_z.append(step_z)
    by_y.append(step_y)
    step_z, step_y = hop(by_z[-1], False), hop(by_y[-1], True)
    lead_factor, inverse = lead_end(work, upper)
    inverse, step_z, step_y = lax.optimization_barrier((inverse, step_z, step_y))
    pieces = by_z + [step_z] + by_y + [step_y]
    sums_other = ring_sums(info_other, slots, padded, pieces)
    moved = swap(sums_other, "row", 1)
    sums = ring_sums(info_own, slots, padded, pieces)
    far_factor = far(info, slots, sums, moved, blocks, padded, inverse)
    return lead_factor, far_factor


def solution(mesh):
    return jax.shard_map(
        shards,
        mesh=mesh,
        in_specs=(
            P("col", None, None),
            P(),
            P(),
            P(("row", "col"), None),
            P(("row", "col"), None),
            P(("row", "col"), None),
            P(("row", "col")),
        ),
        out_specs=(P(), P(("row", "col"), None)),
        check_vma=False,
    )
```

```python
import functools

import jax
import jax.numpy as jnp
from jax import lax
from jax.experimental import pallas as pl
from jax.experimental.pallas import tpu as pltpu
from jax.sharding import PartitionSpec as P

HIGHEST = lax.Precision.HIGHEST
BLOCK = 128
GROUP = 4
SIDE = 4
CACHED = 16
HALF = CACHED // 2
RING = 1


def dot32(left, right):
    return jnp.dot(left, right, precision=HIGHEST, preferred_element_type=jnp.float32)


def spread_rows(value, row):
    return jnp.broadcast_to(value[row : row + 1, :], (8, BLOCK))


def factor_block(block):
    groups = BLOCK // 8
    sub = lax.broadcasted_iota(jnp.int32, (8, BLOCK), 0)
    lane = lax.broadcasted_iota(jnp.int32, (8, BLOCK), 1)
    main = [block[8 * g : 8 * g + 8, :] for g in range(groups)]
    side = [(lane == sub + 8 * g).astype(jnp.float32) for g in range(groups)]
    for panel in range(groups):
        start = 8 * panel
        cols = {
            (g, m): jnp.broadcast_to(main[g][:, start + m : start + m + 1], (8, BLOCK))
            for g in range(panel, groups)
            for m in range(8)
        }
        scale = jnp.ones((8, BLOCK), jnp.float32)
        for j in range(8):
            pivots = {m: spread_rows(cols[panel, m], j) for m in range(j, 8)}
            root = lax.rsqrt(pivots[j])
            root = root * (1.5 - 0.5 * pivots[j] * root * root)
            inverse = root * root
            scale = jnp.where(sub == j, root, scale)
            main_row = spread_rows(main[panel], j)
            side_row = spread_rows(side[panel], j)
            for g in range(panel, groups):
                ratio = cols[g, j] * inverse
                if g == panel:
                    ratio = jnp.where(sub > j, ratio, 0.0)
                for m in range(j + 1, 8):
                    cols[g, m] = cols[g, m] - ratio * pivots[m]
                main[g] = main[g] - ratio * main_row
                side[g] = side[g] - ratio * side_row
        main[panel] = main[panel] * scale
        side[panel] = side[panel] * scale
    for g in range(groups):
        main[g] = jnp.where(lane >= sub + 8 * g, main[g], 0.0)
        side[g] = jnp.where(lane <= sub + 8 * g, side[g], 0.0)
    return jnp.concatenate(main, axis=0), jnp.concatenate(side, axis=0)


def factor_steps(work, upper, begin, end):
    whole = upper.shape[0]
    rows = lax.broadcasted_iota(jnp.int32, (BLOCK, whole), 0)
    columns = lax.broadcasted_iota(jnp.int32, (BLOCK, whole), 1)

    def step(b, carry):
        base = pl.multiple_of(b * BLOCK, BLOCK)
        own = pl.ds(base, BLOCK)
        _, turned = factor_block(work[own, own])
        solved = dot32(turned, work[own, :])
        solved_main = jnp.where(columns >= base + rows, solved[:, :whole], 0.0)
        upper[own, :] = solved_main
        work[own, whole:] = solved[:, whole:]
        below = jnp.where(columns >= base + BLOCK, solved_main, 0.0)
        change = dot32(below.T, jnp.concatenate([below, solved[:, whole:]], axis=1))
        work[...] = work[...] - change
        return carry

    lax.fori_loop(begin, end, step, 0)


def lead_start_kernel(pairs_ref, near_ref, turned_ref, diag_ref, work, upper):
    near_total, size, _ = near_ref.shape
    whole = 2 * size
    first_sums = [sum(pairs_ref[j, k] for k in range(near_total)) for j in range(near_total)]
    second_sums = [sum(pairs_ref[j, k] for j in range(near_total)) for k in range(near_total)]
    work[...] = jnp.zeros_like(work)
    for j in range(near_total):
        left = turned_ref[j]
        mixed = jnp.zeros((size, size), jnp.float32)
        for k in range(near_total):
            product = jnp.dot(left, near_ref[k], preferred_element_type=jnp.float32)
            mixed = mixed + pairs_ref[j, k] * product
            if k == j:
                own = product
        work[:size, :size] += first_sums[j] * own
        work[size:, size:whole] += second_sums[j] * own
        work[:size, size:whole] += mixed
    rows = lax.broadcasted_iota(jnp.int32, (whole, whole), 0)
    columns = lax.broadcasted_iota(jnp.int32, (whole, whole), 1)
    same = rows == columns
    work[:, :whole] += jnp.where(same, jnp.broadcast_to(diag_ref[...], (whole, whole)), 0.0)
    work[:, whole:] = same.astype(jnp.float32)
    factor_steps(work, upper, 0, size // BLOCK)


def lead_end_kernel(work_ref, upper_ref, factor_ref, inverse_ref, work, upper):
    whole = upper.shape[0]
    half = whole // 2
    work[...] = work_ref[...]
    upper[:half, :] = upper_ref[:half, :]
    factor_steps(work, upper, half // BLOCK, whole // BLOCK)
    factor_ref[...] = upper[...].T
    inverse_ref[...] = work[:, whole:].T


VMEM = pl.BlockSpec(memory_space=pltpu.VMEM)


def lead_start(pairs, near_cache, turned_near, lead_diag):
    whole = lead_diag.shape[0]
    return pl.pallas_call(
        lead_start_kernel,
        out_shape=(
            jax.ShapeDtypeStruct((whole, 2 * whole), jnp.float32),
            jax.ShapeDtypeStruct((whole, whole), jnp.float32),
        ),
        in_specs=[pl.BlockSpec(memory_space=pltpu.SMEM), VMEM, VMEM, VMEM],
        out_specs=(VMEM, VMEM),
        compiler_params=pltpu.CompilerParams(vmem_limit_bytes=24 << 20),
        cost_estimate=pl.CostEstimate(
            flops=9_000_000_000, bytes_accessed=6 << 20, transcendentals=0
        ),
        name="lead_start",
    )(pairs, near_cache, turned_near, lead_diag.reshape(1, whole))


def lead_end(work, upper):
    whole = upper.shape[0]
    square = jax.ShapeDtypeStruct((whole, whole), jnp.float32)
    return pl.pallas_call(
        lead_end_kernel,
        out_shape=(square, square),
        in_specs=[VMEM, VMEM],
        out_specs=(VMEM, VMEM),
        scratch_shapes=[
            pltpu.VMEM((whole, 2 * whole), jnp.float32),
            pltpu.VMEM((whole, whole), jnp.float32),
        ],
        compiler_params=pltpu.CompilerParams(vmem_limit_bytes=24 << 20),
        cost_estimate=pl.CostEstimate(
            flops=9_000_000_000, bytes_accessed=6 << 20, transcendentals=0
        ),
        name="lead_end",
    )(work, upper)


def ring_places(offsets, core, y, z):
    col, local = offsets // CACHED, offsets % CACHED
    half, inner = local // HALF, local % HALF
    sign = 1 - 2 * core
    from_y = (sign * (y - col // SIDE)) & (SIDE - 1)
    from_z = (sign * (z - col % SIDE)) & (SIDE - 1)
    by_z = inner < RING
    major = jnp.where(by_z, from_z, from_y)
    minor = jnp.where(by_z, from_y, from_z)
    place = jnp.where(by_z, inner, inner - RING + SIDE * SIDE * RING)
    held = (half == core) & (inner < 2 * RING)
    return jnp.where(held, (major * SIDE + minor) * RING + place, -1)


def spread_places(offsets):
    col, local = offsets // CACHED, offsets % CACHED
    half, inner = local // HALF, local % HALF
    kept = HALF - 2 * RING
    place = col * (2 * kept) + half * kept + inner - 2 * RING
    return jnp.where(inner >= 2 * RING, place, -1)


def list_slots(tile, info_ref, items, slots):
    def visit(s, count):
        place = info_ref[tile, s]
        items[0, tile, count] = place
        items[1, tile, count] = info_ref[tile, slots + s]
        items[2, tile, count] = info_ref[tile, 2 * slots + s]
        return count + (place >= 0).astype(jnp.int32)

    return lax.fori_loop(0, slots, visit, 0)


def left_rows(tile, r, count, items, turned_ref):
    empty = turned_ref.shape[0] - 1
    firsts, seconds = [], []
    for i in range(GROUP):
        q = r * GROUP + i
        used = q < count
        firsts.append(turned_ref[jnp.where(used, items[1, tile, q], empty)])
        seconds.append(turned_ref[jnp.where(used, items[2, tile, q], empty)])
    return jnp.concatenate(
        [jnp.concatenate(firsts, axis=1), jnp.concatenate(seconds, axis=1)], axis=0
    )


def ring_kernel(slots, info_ref, turned_ref, *refs):
    *pieces, out_ref, held, items, arrived = refs
    size = turned_ref.shape[1]
    tile = pl.program_id(0)
    copies = []
    start = 0
    for n, piece in enumerate(pieces):
        copies.append(
            pltpu.make_async_copy(piece, held.at[pl.ds(start, piece.shape[0])], arrived.at[n])
        )
        start += piece.shape[0]

    @pl.when(tile == 0)
    def fetch():
        for copy in copies:
            copy.start()

    count = list_slots(tile, info_ref, items, slots)

    @pl.when(tile == 0)
    def wait():
        for copy in copies:
            copy.wait()

    out_ref[...] = jnp.zeros_like(out_ref)

    def one_round(r, carry):
        rights = []
        for i in range(GROUP):
            q = r * GROUP + i
            rights.append(held[jnp.where(q < count, items[0, tile, q], 0)])
        out_ref[0] += jnp.dot(
            left_rows(tile, r, count, items, turned_ref),
            jnp.concatenate(rights, axis=0),
            preferred_element_type=jnp.float32,
        )
        return carry

    lax.fori_loop(0, (count + GROUP - 1) // GROUP, one_round, 0)


def ring_sums(info, slots, turned_near, pieces):
    tiles = info.shape[0]
    size = turned_near.shape[1]
    per_tile = pl.BlockSpec((1, 2 * size, size), lambda t, *_: (t, 0, 0))
    return pl.pallas_call(
        functools.partial(ring_kernel, slots),
        out_shape=jax.ShapeDtypeStruct((tiles, 2 * size, size), jnp.float32),
        grid_spec=pltpu.PrefetchScalarGridSpec(
            num_scalar_prefetch=1,
            grid=(tiles,),
            in_specs=[pl.BlockSpec(turned_near.shape, lambda t, *_: (0, 0, 0))]
            + [pl.BlockSpec(memory_space=pltpu.HBM)] * len(pieces),
            out_specs=per_tile,
            scratch_shapes=[
                pltpu.VMEM((sum(p.shape[0] for p in pieces), size, size), jnp.bfloat16),
                pltpu.SMEM((3, tiles, slots), jnp.int32),
                pltpu.SemaphoreType.DMA((len(pieces),)),
            ],
        ),
        compiler_params=pltpu.CompilerParams(
            dimension_semantics=("arbitrary",), vmem_limit_bytes=60 << 20
        ),
        cost_estimate=pl.CostEstimate(
            flops=3_000_000_000, bytes_accessed=12 << 20, transcendentals=0
        ),
        name="ring_sums",
    )(info, turned_near, *pieces)


def far_kernel(
    slots, info_ref, own_hbm, other_hbm, blocks_ref, turned_hbm, inverse_hbm, out_hbm, held, total,
    other_ref, turned_ref, inverse_ref, out_ref, items, arrived, loaded, stored,
):
    tiles = info_ref.shape[0]
    size = turned_ref.shape[1]
    span = GROUP * size

    def fetch(t, q, place):
        return pltpu.make_async_copy(
            blocks_ref.at[place],
            held.at[t, pl.ds(pl.multiple_of(q * size, size), size), :],
            arrived.at[t, q],
        )

    def store(t):
        return pltpu.make_async_copy(
            out_ref.at[t], out_hbm.at[pl.ds(t * size, size), :], stored.at[t]
        )

    load_turned = pltpu.make_async_copy(turned_hbm, turned_ref, loaded.at[0])
    load_own = pltpu.make_async_copy(own_hbm, total, loaded.at[1])
    load_inverse = pltpu.make_async_copy(inverse_hbm, inverse_ref, loaded.at[2])
    load_other = pltpu.make_async_copy(other_hbm, other_ref, loaded.at[3])
    load_turned.start()
    load_own.start()
    counts = []
    for t in range(tiles):
        count = list_slots(t, info_ref, items, slots)
        counts.append(count)

        def begin(q, carry):
            fetch(t, q, jnp.where(q < count, items[0, t, q], 0)).start()
            return carry

        lax.fori_loop(0, (count + GROUP - 1) // GROUP * GROUP, begin, 0)
    load_other.start()
    load_inverse.start()
    load_turned.wait()
    load_own.wait()
    for t in range(tiles):

        def one_round(r, carry):
            for i in range(GROUP):
                fetch(t, r * GROUP + i, 0).wait()
            right = held[t, pl.ds(pl.multiple_of(r * span, span), span), :]
            total[t] += jnp.dot(
                left_rows(t, r, counts[t], items, turned_ref),
                right,
                preferred_element_type=jnp.float32,
            )
            return carry

        lax.fori_loop(0, (counts[t] + GROUP - 1) // GROUP, one_round, 0)
        if t == 0:
            load_other.wait()
            load_inverse.wait()
        turned = (total[t] + other_ref[t]).T
        out_ref[t, :, :size] = dot32(turned[:, :size], inverse_ref[:size, :size])
        out_ref[t, :, size:] = dot32(turned, inverse_ref[:, size:])
        store(t).start()
    for t in range(tiles):
        store(t).wait()


HBM = pl.BlockSpec(memory_space=pltpu.HBM)


def far(info, slots, sums, other_sums, blocks, turned_near, inverse):
    tiles = info.shape[0]
    size = blocks.shape[1]
    return pl.pallas_call(
        functools.partial(far_kernel, slots),
        out_shape=jax.ShapeDtypeStruct((tiles * size, 2 * size), jnp.float32),
        in_specs=[pl.BlockSpec(memory_space=pltpu.SMEM)] + [HBM] * 5,
        out_specs=HBM,
        scratch_shapes=[
            pltpu.VMEM((tiles, slots * size, size), jnp.bfloat16),
            pltpu.VMEM(sums.shape, jnp.float32),
            pltpu.VMEM(sums.shape, jnp.float32),
            pltpu.VMEM(turned_near.shape, jnp.bfloat16),
            pltpu.VMEM(inverse.shape, jnp.float32),
            pltpu.VMEM((tiles, size, 2 * size), jnp.float32),
            pltpu.SMEM((3, tiles, slots), jnp.int32),
            pltpu.SemaphoreType.DMA((tiles, slots)),
            pltpu.SemaphoreType.DMA((4,)),
            pltpu.SemaphoreType.DMA((tiles,)),
        ],
        compiler_params=pltpu.CompilerParams(vmem_limit_bytes=63 << 20),
        name="far",
    )(info, sums, other_sums, blocks, turned_near, inverse)


def local_pairs(near_first, near_second, counts, near_total):
    slots = near_first.shape[1]
    usable = jnp.arange(slots, dtype=jnp.int32)[None, :] < counts[:, None]
    labels = jnp.arange(near_total, dtype=jnp.int32)
    first_hot = (near_first[:, :, None] == labels) & usable[:, :, None]
    second_hot = near_second[:, :, None] == labels
    both = first_hot[:, :, :, None] & second_hot[:, :, None, :]
    return jnp.sum(both.astype(jnp.float32), axis=(0, 1))


def hop(value, along_y):
    rows, cols = lax.axis_size("row"), lax.axis_size("col")
    moves = []
    for row in range(rows):
        sign = 1 - 2 * (row % 2)
        for col in range(cols):
            y, z = col // SIDE, col % SIDE
            y, z = ((y + sign) % SIDE, z) if along_y else (y, (z + sign) % SIDE)
            moves.append((row * cols + col, row * cols + y * SIDE + z))
    return lax.ppermute(value, ("row", "col"), moves)


def swap(value, axis, bit):
    return lax.ppermute(value, axis, [(i, i ^ bit) for i in range(lax.axis_size(axis))])


def shards(
    response_cache, near_cache, lead_diag, far_offsets, near_first, near_second, tile_counts
):
    near_total = near_cache.shape[0]
    slots = far_offsets.shape[1]
    row = lax.axis_index("row")
    core = row % 2
    kept = HALF - 2 * RING
    size = near_cache.shape[1]
    share = 2 * kept * size // lax.axis_size("row")
    at = row * share
    own = lax.dynamic_slice_in_dim(
        response_cache.reshape(CACHED * size, size),
        at // (kept * size) * HALF * size + 2 * RING * size + at % (kept * size),
        share,
        0,
    )
    blocks = lax.all_gather(own, ("col", "row"), axis=0, tiled=True).reshape(-1, size, size)
    line_y = [lax.dynamic_slice_in_dim(response_cache, core * HALF, RING, 0)]
    line_z = [lax.dynamic_slice_in_dim(response_cache, core * HALF + RING, RING, 0)]
    usable = jnp.arange(slots, dtype=jnp.int32)[None, :] < tile_counts[:, None]
    y, z = lax.axis_index("col") // SIDE, lax.axis_index("col") % SIDE
    info, info_own, info_other = (
        jnp.concatenate([jnp.where(usable, places, -1), near_first, near_second], axis=1)
        for places in (
            spread_places(far_offsets),
            ring_places(far_offsets, core, y, z),
            ring_places(far_offsets, 1 - core, y, z),
        )
    )
    turned = jnp.transpose(near_cache, (0, 2, 1))
    padded = jnp.concatenate([turned, jnp.zeros_like(turned[:1])], axis=0)
    pairs = local_pairs(near_first, near_second, tile_counts, near_total)

    def advance(pairs, rings, stages):
        (to_z, along_y), (to_y, along_z) = rings
        to_z, to_y = hop(to_z, along_y), hop(to_y, along_z)
        for axis, bit in stages:
            pairs = pairs + swap(pairs, axis, bit)
        return lax.optimization_barrier((pairs, to_z, to_y))

    for stages in (
        (("row", 1), ("row", 4), ("row", 2)),
        (("col", 8), ("col", 4)),
        (("col", 2), ("col", 1)),
    ):
        pairs, step_y, step_z = advance(
            pairs, ((line_y[-1], True), (line_z[-1], False)), stages
        )
        line_y.append(step_y)
        line_z.append(step_z)
    by_z = [jnp.concatenate(line_y, axis=0)]
    by_y = [jnp.concatenate(line_z, axis=0)]
    for _ in range(2):
        pairs, step_z, step_y = advance(pairs, ((by_z[-1], False), (by_y[-1], True)), ())
        by_z.append(step_z)
        by_y.append(step_y)
    step_z, step_y = hop(by_z[-1], False), hop(by_y[-1], True)
    info_other = swap(info_other, "row", 1)
    work, upper = lead_start(pairs, near_cache, turned, lead_diag)
    lead_factor, inverse = lead_end(work, upper)
    inverse, step_z, step_y = lax.optimization_barrier((inverse, step_z, step_y))
    pieces = by_z + [step_z] + by_y + [step_y]
    sums_other = ring_sums(info_other, slots, padded, pieces)
    moved = swap(sums_other, "row", 1)
    sums = ring_sums(info_own, slots, padded, pieces)
    far_factor = far(info, slots, sums, moved, blocks, padded, inverse)
    return lead_factor, far_factor


def solution(mesh):
    return jax.shard_map(
        shards,
        mesh=mesh,
        in_specs=(
            P("col", None, None),
            P(),
            P(),
            P(("row", "col"), None),
            P(("row", "col"), None),
            P(("row", "col"), None),
            P(("row", "col")),
        ),
        out_specs=(P(), P(("row", "col"), None)),
        check_vma=False,
    )
```

```python
import functools

import jax
import jax.numpy as jnp
from jax import lax
from jax.experimental import pallas as pl
from jax.experimental.pallas import tpu as pltpu
from jax.sharding import PartitionSpec as P

HIGHEST = lax.Precision.HIGHEST
BLOCK = 128
GROUP = 12
AHEAD = 2


def dot32(left, right):
    return jnp.dot(left, right, precision=HIGHEST, preferred_element_type=jnp.float32)


def split3(value):
    high = value.astype(jnp.bfloat16)
    rest = value - high.astype(jnp.float32)
    middle = rest.astype(jnp.bfloat16)
    low = (rest - middle.astype(jnp.float32)).astype(jnp.bfloat16)
    return high, middle, low


def spread_rows(value, row):
    return jnp.broadcast_to(value[row : row + 1, :], (8, BLOCK))


def factor_block(block):
    groups = BLOCK // 8
    sub = lax.broadcasted_iota(jnp.int32, (8, BLOCK), 0)
    lane = lax.broadcasted_iota(jnp.int32, (8, BLOCK), 1)
    main = [block[8 * g : 8 * g + 8, :] for g in range(groups)]
    side = [(lane == sub + 8 * g).astype(jnp.float32) for g in range(groups)]
    for panel in range(groups):
        start = 8 * panel
        cols = {
            (g, m): jnp.broadcast_to(main[g][:, start + m : start + m + 1], (8, BLOCK))
            for g in range(panel, groups)
            for m in range(8)
        }
        scale = jnp.ones((8, BLOCK), jnp.float32)
        for j in range(8):
            pivots = {m: spread_rows(cols[panel, m], j) for m in range(j, 8)}
            root = lax.rsqrt(pivots[j])
            root = root * (1.5 - 0.5 * pivots[j] * root * root)
            inverse = root * root
            scale = jnp.where(sub == j, root, scale)
            main_row = spread_rows(main[panel], j)
            side_row = spread_rows(side[panel], j)
            for g in range(panel, groups):
                ratio = cols[g, j] * inverse
                if g == panel:
                    ratio = jnp.where(sub > j, ratio, 0.0)
                for m in range(j + 1, 8):
                    cols[g, m] = cols[g, m] - ratio * pivots[m]
                main[g] = main[g] - ratio * main_row
                side[g] = side[g] - ratio * side_row
        main[panel] = main[panel] * scale
        side[panel] = side[panel] * scale
    for g in range(groups):
        main[g] = jnp.where(lane >= sub + 8 * g, main[g], 0.0)
        side[g] = jnp.where(lane <= sub + 8 * g, side[g], 0.0)
    return jnp.concatenate(main, axis=0), jnp.concatenate(side, axis=0)


def lead_kernel(pairs_ref, near_ref, turned_ref, diag_ref, factor_ref, parts_ref, work, upper):
    near_total, size, _ = near_ref.shape
    whole = 2 * size
    first_sums = [sum(pairs_ref[j, k] for k in range(near_total)) for j in range(near_total)]
    second_sums = [sum(pairs_ref[j, k] for j in range(near_total)) for k in range(near_total)]
    work[...] = jnp.zeros_like(work)
    for j in range(near_total):
        left = turned_ref[j]
        mixed = jnp.zeros((size, size), jnp.float32)
        for k in range(near_total):
            product = jnp.dot(left, near_ref[k], preferred_element_type=jnp.float32)
            mixed = mixed + pairs_ref[j, k] * product
            if k == j:
                own = product
        work[:size, :size] += first_sums[j] * own
        work[size:, size:whole] += second_sums[j] * own
        work[:size, size:whole] += mixed
    rows = lax.broadcasted_iota(jnp.int32, (whole, whole), 0)
    columns = lax.broadcasted_iota(jnp.int32, (whole, whole), 1)
    same = rows == columns
    work[:, :whole] += jnp.where(same, jnp.broadcast_to(diag_ref[...], (whole, whole)), 0.0)
    work[:, whole:] = same.astype(jnp.float32)

    def step(b, carry):
        base = pl.multiple_of(b * BLOCK, BLOCK)
        own = pl.ds(base, BLOCK)
        _, turned = factor_block(work[own, own])
        solved = dot32(turned, work[own, :])
        at = columns[:BLOCK, :] >= base + rows[:BLOCK, :]
        solved_main = jnp.where(at, solved[:, :whole], 0.0)
        upper[own, :] = solved_main
        work[own, whole:] = solved[:, whole:]
        below = jnp.where(columns[:BLOCK, :] >= base + BLOCK, solved_main, 0.0)
        change = dot32(below.T, jnp.concatenate([below, solved[:, whole:]], axis=1))
        work[...] = work[...] - change
        return carry

    lax.fori_loop(0, whole // BLOCK, step, 0)
    factor_ref[...] = upper[...].T
    high, middle, low = split3(work[:, whole:].T)
    for n, part in enumerate((high, middle, high, low, middle, high)):
        parts_ref[n * size : (n + 1) * size, :] = part[:size, :size]
        parts_ref[(6 + 2 * n) * size : (8 + 2 * n) * size, :] = part[:, size:]


def lead(pairs, near_cache, turned_near, lead_diag):
    whole = lead_diag.shape[0]
    vmem = pl.BlockSpec(memory_space=pltpu.VMEM)
    return pl.pallas_call(
        lead_kernel,
        out_shape=(
            jax.ShapeDtypeStruct((whole, whole), jnp.float32),
            jax.ShapeDtypeStruct((9 * whole, whole // 2), jnp.bfloat16),
        ),
        in_specs=[pl.BlockSpec(memory_space=pltpu.SMEM), vmem, vmem, vmem],
        out_specs=(vmem, vmem),
        scratch_shapes=[
            pltpu.VMEM((whole, 2 * whole), jnp.float32),
            pltpu.VMEM((whole, whole), jnp.float32),
        ],
        compiler_params=pltpu.CompilerParams(vmem_limit_bytes=40 << 20),
        name="lead",
    )(pairs, near_cache, turned_near, lead_diag.reshape(1, whole))


def far_kernel(
    slots, info_ref, blocks_ref, near_hbm, parts_hbm, out_hbm, held, near_ref, parts_ref, out_ref,
    arrived, loaded, stored,
):
    tiles = info_ref.shape[0]
    size = near_ref.shape[1]
    rounds = slots // GROUP
    last = tiles * rounds

    def begin(k):
        t, r = k // rounds, k % rounds
        for i in range(GROUP):
            pltpu.make_async_copy(
                blocks_ref.at[info_ref[t, r * GROUP + i]], held.at[k, i], arrived.at[k]
            ).start()

    def finish(k):
        pltpu.make_async_copy(blocks_ref.at[pl.ds(0, GROUP)], held.at[k], arrived.at[k]).wait()

    def store(t):
        rows = pl.ds(pl.multiple_of(t * size, size), size)
        return pltpu.make_async_copy(out_ref.at[t], out_hbm.at[rows, :], stored.at[t])

    load_near = pltpu.make_async_copy(near_hbm, near_ref, loaded.at[0])
    load_parts = pltpu.make_async_copy(parts_hbm, parts_ref, loaded.at[1])
    load_near.start()
    for k in range(AHEAD):
        begin(k)
    load_parts.start()
    load_near.wait()

    def step(k, carry):
        @pl.when(k + AHEAD < last)
        def following():
            begin(k + AHEAD)

        t, r = k // rounds, k % rounds
        finish(k)
        rows = []
        for i in range(GROUP):
            s = r * GROUP + i
            rows.append(
                jnp.concatenate(
                    [near_ref[info_ref[t, slots + s]], near_ref[info_ref[t, 2 * slots + s]]],
                    axis=1,
                )
            )
        change = lax.dot_general(
            held[k].reshape(GROUP * size, size),
            jnp.concatenate(rows, axis=0),
            (((0,), (0,)), ((), ())),
            preferred_element_type=jnp.float32,
        )

        @pl.when(r == 0)
        def first():
            out_ref[t] = change

        @pl.when(r > 0)
        def later():
            out_ref[t] += change

        @pl.when(k == 0)
        def factors():
            load_parts.wait()

        @pl.when(r == rounds - 1)
        def solve():
            high, middle, low = split3(out_ref[t])
            wide = jnp.concatenate([high, high, middle, high, middle, low], axis=1)
            narrow = jnp.concatenate(
                [p[:, :size] for p in (high, high, middle, high, middle, low)], axis=1
            )
            out_ref[t, :, :size] = jnp.dot(
                narrow, parts_ref[: 6 * size, :], preferred_element_type=jnp.float32
            )
            out_ref[t, :, size:] = jnp.dot(
                wide, parts_ref[6 * size :, :], preferred_element_type=jnp.float32
            )
            store(t).start()

        return carry

    lax.fori_loop(0, last, step, 0)
    for t in range(tiles):
        store(t).wait()


def far(info, blocks, near, parts):
    tiles = info.shape[0]
    slots = info.shape[1] // 3
    size = blocks.shape[1]
    rounds = tiles * slots // GROUP
    hbm = pl.BlockSpec(memory_space=pltpu.HBM)
    return pl.pallas_call(
        functools.partial(far_kernel, slots),
        out_shape=jax.ShapeDtypeStruct((tiles * size, 2 * size), jnp.float32),
        in_specs=[pl.BlockSpec(memory_space=pltpu.SMEM), hbm, hbm, hbm],
        out_specs=hbm,
        scratch_shapes=[
            pltpu.VMEM((rounds, GROUP, size, size), jnp.bfloat16),
            pltpu.VMEM(near.shape, jnp.bfloat16),
            pltpu.VMEM(parts.shape, jnp.bfloat16),
            pltpu.VMEM((tiles, size, 2 * size), jnp.float32),
            pltpu.SemaphoreType.DMA((rounds,)),
            pltpu.SemaphoreType.DMA((2,)),
            pltpu.SemaphoreType.DMA((tiles,)),
        ],
        compiler_params=pltpu.CompilerParams(vmem_limit_bytes=63 << 20),
        name="far",
    )(info, blocks, near, parts)


def local_pairs(near_first, near_second, counts, near_total):
    slots = near_first.shape[1]
    usable = jnp.arange(slots, dtype=jnp.int32)[None, :] < counts[:, None]
    labels = jnp.arange(near_total, dtype=jnp.int32)
    first_hot = (near_first[:, :, None] == labels) & usable[:, :, None]
    second_hot = near_second[:, :, None] == labels
    both = first_hot[:, :, :, None] & second_hot[:, :, None, :]
    return jnp.sum(both.astype(jnp.float32), axis=(0, 1))


def total_pairs(value):
    for axis, bits in (("row", (1, 4, 2)), ("col", (8, 4, 2, 1))):
        size = lax.axis_size(axis)
        for bit in bits:
            value = value + lax.ppermute(value, axis, [(i, i ^ bit) for i in range(size)])
    return value


def shards(
    response_cache, near_cache, lead_diag, far_offsets, near_first, near_second, tile_counts
):
    near_total = near_cache.shape[0]
    cached, size = response_cache.shape[:2]
    share = cached * size // lax.axis_size("row")
    own = lax.dynamic_slice_in_dim(
        response_cache.reshape(cached * size, size), lax.axis_index("row") * share, share, 0
    )
    blocks = lax.all_gather(own, ("col", "row"), axis=0, tiled=True).reshape(-1, size, size)
    pairs = total_pairs(local_pairs(near_first, near_second, tile_counts, near_total))
    turned = jnp.transpose(near_cache, (0, 2, 1))
    padded = jnp.concatenate([near_cache, jnp.zeros_like(near_cache[:1])], axis=0)
    lead_factor, parts = lead(pairs, near_cache, turned, lead_diag)
    usable = jnp.arange(far_offsets.shape[1], dtype=jnp.int32)[None, :] < tile_counts[:, None]
    info = jnp.concatenate(
        [far_offsets]
        + [jnp.where(usable, labels, near_total) for labels in (near_first, near_second)],
        axis=1,
    )
    far_factor = far(info, blocks, padded, parts)
    return lead_factor, far_factor


def solution(mesh):
    return jax.shard_map(
        shards,
        mesh=mesh,
        in_specs=(
            P("col", None, None),
            P(),
            P(),
            P(("row", "col"), None),
            P(("row", "col"), None),
            P(("row", "col"), None),
            P(("row", "col")),
        ),
        out_specs=(P(), P(("row", "col"), None)),
        check_vma=False,
    )
```

```python
import functools

import jax
import jax.numpy as jnp
from jax import lax
from jax.experimental import pallas as pl
from jax.experimental.pallas import tpu as pltpu
from jax.sharding import PartitionSpec as P

HIGHEST = lax.Precision.HIGHEST
BLOCK = 128
GROUP = 4


def dot32(left, right):
    return jnp.dot(left, right, precision=HIGHEST, preferred_element_type=jnp.float32)


def split3(value):
    high = value.astype(jnp.bfloat16)
    rest = value - high.astype(jnp.float32)
    middle = rest.astype(jnp.bfloat16)
    low = (rest - middle.astype(jnp.float32)).astype(jnp.bfloat16)
    return high, middle, low


def spread_rows(value, row):
    return jnp.broadcast_to(value[row : row + 1, :], (8, BLOCK))


def factor_block(block):
    groups = BLOCK // 8
    sub = lax.broadcasted_iota(jnp.int32, (8, BLOCK), 0)
    lane = lax.broadcasted_iota(jnp.int32, (8, BLOCK), 1)
    main = [block[8 * g : 8 * g + 8, :] for g in range(groups)]
    side = [(lane == sub + 8 * g).astype(jnp.float32) for g in range(groups)]
    for panel in range(groups):
        start = 8 * panel
        cols = {
            (g, m): jnp.broadcast_to(main[g][:, start + m : start + m + 1], (8, BLOCK))
            for g in range(panel, groups)
            for m in range(8)
        }
        scale = jnp.ones((8, BLOCK), jnp.float32)
        for j in range(8):
            pivots = {m: spread_rows(cols[panel, m], j) for m in range(j, 8)}
            root = lax.rsqrt(pivots[j])
            root = root * (1.5 - 0.5 * pivots[j] * root * root)
            inverse = root * root
            scale = jnp.where(sub == j, root, scale)
            main_row = spread_rows(main[panel], j)
            side_row = spread_rows(side[panel], j)
            for g in range(panel, groups):
                ratio = cols[g, j] * inverse
                if g == panel:
                    ratio = jnp.where(sub > j, ratio, 0.0)
                for m in range(j + 1, 8):
                    cols[g, m] = cols[g, m] - ratio * pivots[m]
                main[g] = main[g] - ratio * main_row
                side[g] = side[g] - ratio * side_row
        main[panel] = main[panel] * scale
        side[panel] = side[panel] * scale
    for g in range(groups):
        main[g] = jnp.where(lane >= sub + 8 * g, main[g], 0.0)
        side[g] = jnp.where(lane <= sub + 8 * g, side[g], 0.0)
    return jnp.concatenate(main, axis=0), jnp.concatenate(side, axis=0)


def lead_kernel(pairs_ref, near_ref, turned_ref, diag_ref, factor_ref, parts_ref, work, upper):
    near_total, size, _ = near_ref.shape
    whole = 2 * size
    first_sums = [sum(pairs_ref[j, k] for k in range(near_total)) for j in range(near_total)]
    second_sums = [sum(pairs_ref[j, k] for j in range(near_total)) for k in range(near_total)]
    work[...] = jnp.zeros_like(work)
    for j in range(near_total):
        left = turned_ref[j]
        mixed = jnp.zeros((size, size), jnp.float32)
        for k in range(near_total):
            product = jnp.dot(left, near_ref[k], preferred_element_type=jnp.float32)
            mixed = mixed + pairs_ref[j, k] * product
            if k == j:
                own = product
        work[:size, :size] += first_sums[j] * own
        work[size:, size:whole] += second_sums[j] * own
        work[:size, size:whole] += mixed
    rows = lax.broadcasted_iota(jnp.int32, (whole, whole), 0)
    columns = lax.broadcasted_iota(jnp.int32, (whole, whole), 1)
    same = rows == columns
    work[:, :whole] += jnp.where(same, jnp.broadcast_to(diag_ref[...], (whole, whole)), 0.0)
    work[:, whole:] = same.astype(jnp.float32)

    def step(b, carry):
        base = pl.multiple_of(b * BLOCK, BLOCK)
        own = pl.ds(base, BLOCK)
        _, turned = factor_block(work[own, own])
        solved = dot32(turned, work[own, :])
        at = columns[:BLOCK, :] >= base + rows[:BLOCK, :]
        solved_main = jnp.where(at, solved[:, :whole], 0.0)
        upper[own, :] = solved_main
        work[own, whole:] = solved[:, whole:]
        below = jnp.where(columns[:BLOCK, :] >= base + BLOCK, solved_main, 0.0)
        change = dot32(below.T, jnp.concatenate([below, solved[:, whole:]], axis=1))
        work[...] = work[...] - change
        return carry

    lax.fori_loop(0, whole // BLOCK, step, 0)
    factor_ref[...] = upper[...].T
    high, middle, low = split3(work[:, whole:].T)
    for n, part in enumerate((high, middle, low)):
        for half in range(2):
            for columns in range(2):
                parts_ref[n, half, columns] = part[
                    half * size : (half + 1) * size, columns * size : (columns + 1) * size
                ]


def lead(pairs, near_cache, turned_near, lead_diag):
    whole = lead_diag.shape[0]
    vmem = pl.BlockSpec(memory_space=pltpu.VMEM)
    return pl.pallas_call(
        lead_kernel,
        out_shape=(
            jax.ShapeDtypeStruct((whole, whole), jnp.float32),
            jax.ShapeDtypeStruct((3, 2, 2, whole // 2, whole // 2), jnp.bfloat16),
        ),
        in_specs=[pl.BlockSpec(memory_space=pltpu.SMEM), vmem, vmem, vmem],
        out_specs=(vmem, vmem),
        scratch_shapes=[
            pltpu.VMEM((whole, 2 * whole), jnp.float32),
            pltpu.VMEM((whole, whole), jnp.float32),
        ],
        compiler_params=pltpu.CompilerParams(vmem_limit_bytes=40 << 20),
        name="lead",
    )(pairs, near_cache, turned_near, lead_diag.reshape(1, whole))


def far_kernel(
    slots, sums, info_ref, blocks_ref, turned_hbm, parts_hbm, out_hbm, held, turned_ref, parts_ref,
    out_ref, arrived, loaded, stored,
):
    tiles = info_ref.shape[0]
    size = turned_ref.shape[1]

    def rounds_of(t):
        return (info_ref[t, 3 * slots] + GROUP - 1) // GROUP

    def begin(t, r):
        for i in range(GROUP):
            s = r * GROUP + i
            pltpu.make_async_copy(
                blocks_ref.at[info_ref[t, s]], held.at[t, s], arrived.at[t, r]
            ).start()

    def begin_rounds(t, first, past):
        def begin_round(r, carry):
            begin(t, r)
            return carry

        lax.fori_loop(first, past, begin_round, 0)

    def finish(t, r):
        pltpu.make_async_copy(
            blocks_ref.at[pl.ds(0, GROUP)],
            held.at[t, pl.ds(r * GROUP, GROUP)],
            arrived.at[t, r],
        ).wait()

    def store(t):
        rows = pl.ds(pl.multiple_of(t * size, size), size)
        return pltpu.make_async_copy(out_ref.at[t], out_hbm.at[rows, :], stored.at[t])

    def multiply(total, unit, terms):
        for n, (left, right) in enumerate(terms):
            pltpu.matmul_push_rhs(right, n % 2, unit)
            pltpu.matmul_acc_lhs(total, left, n % 2)

    def main(first_sum, second_sum):
        load_turned = pltpu.make_async_copy(turned_hbm, turned_ref, loaded.at[0])
        load_parts = pltpu.make_async_copy(parts_hbm, parts_ref, loaded.at[1])
        load_turned.start()
        begin_rounds(0, 0, rounds_of(0))
        load_parts.start()
        pltpu.matmul_pop(first_sum)
        pltpu.matmul_pop(second_sum)
        load_turned.wait()

        def tile_step(t, carry):
            rounds = rounds_of(t)
            following = jnp.minimum(t + 1, tiles - 1)
            next_rounds = jnp.where(t + 1 < tiles, rounds_of(following), 0)

            def one_round(r, carry):
                @pl.when(r < next_rounds)
                def fetch():
                    begin(following, r)

                finish(t, r)
                for i in range(GROUP):
                    s = r * GROUP + i
                    block = held[t, s]
                    pltpu.matmul_push_rhs(block, i % 2, 0)
                    pltpu.matmul_push_rhs(block, i % 2, 1)
                    pltpu.matmul_acc_lhs(first_sum, turned_ref[info_ref[t, slots + s]], i % 2)
                    pltpu.matmul_acc_lhs(second_sum, turned_ref[info_ref[t, 2 * slots + s]], i % 2)
                return carry

            lax.fori_loop(0, rounds, one_round, 0)
            begin_rounds(following, rounds, jnp.maximum(rounds, next_rounds))

            @pl.when(t == 0)
            def factors():
                load_parts.wait()

            rows = (
                split3(pltpu.matmul_pop(first_sum).T),
                split3(pltpu.matmul_pop(second_sum).T),
            )
            products = ((0, 0), (0, 1), (1, 0), (0, 2), (1, 1), (2, 0))

            def terms(half, columns, chosen):
                return [(rows[half][i], parts_ref[j, half, columns]) for i, j in chosen]

            multiply(first_sum, 0, terms(0, 0, products))
            multiply(second_sum, 1, terms(0, 1, products) + terms(1, 1, products[3:]))
            out_ref[t, :, :size] = pltpu.matmul_pop(first_sum)
            multiply(first_sum, 0, terms(1, 1, products[:3]))
            out_ref[t, :, size:] = pltpu.matmul_pop(second_sum) + pltpu.matmul_pop(first_sum)
            store(t).start()
            return carry

        lax.fori_loop(0, tiles, tile_step, 0)
        for t in range(tiles):
            store(t).wait()

    pl.run_scoped(main, *sums)


def far(info, blocks, turned_near, parts):
    tiles = info.shape[0]
    slots = info.shape[1] // 3
    size = blocks.shape[1]
    hbm = pl.BlockSpec(memory_space=pltpu.HBM)
    sums = [pltpu.ACC(mxu_id=n)((size, size), jnp.float32) for n in range(2)]
    return pl.pallas_call(
        functools.partial(far_kernel, slots, sums),
        out_shape=jax.ShapeDtypeStruct((tiles * size, 2 * size), jnp.float32),
        in_specs=[pl.BlockSpec(memory_space=pltpu.SMEM), hbm, hbm, hbm],
        out_specs=hbm,
        scratch_shapes=[
            pltpu.VMEM((tiles, slots, size, size), jnp.bfloat16),
            pltpu.VMEM(turned_near.shape, jnp.bfloat16),
            pltpu.VMEM(parts.shape, jnp.bfloat16),
            pltpu.VMEM((tiles, size, 2 * size), jnp.float32),
            pltpu.SemaphoreType.DMA((tiles, slots // GROUP)),
            pltpu.SemaphoreType.DMA((2,)),
            pltpu.SemaphoreType.DMA((tiles,)),
        ],
        compiler_params=pltpu.CompilerParams(vmem_limit_bytes=63 << 20),
        name="far",
    )(info, blocks, turned_near, parts)


def local_pairs(near_first, near_second, counts, near_total):
    slots = near_first.shape[1]
    usable = jnp.arange(slots, dtype=jnp.int32)[None, :] < counts[:, None]
    labels = jnp.arange(near_total, dtype=jnp.int32)
    first_hot = (near_first[:, :, None] == labels) & usable[:, :, None]
    second_hot = near_second[:, :, None] == labels
    both = first_hot[:, :, :, None] & second_hot[:, :, None, :]
    return jnp.sum(both.astype(jnp.float32), axis=(0, 1))


def total_pairs(value):
    for axis, bits in (("row", (1, 4, 2)), ("col", (8, 4, 2, 1))):
        size = lax.axis_size(axis)
        for bit in bits:
            value = value + lax.ppermute(value, axis, [(i, i ^ bit) for i in range(size)])
    return value


def shards(
    response_cache, near_cache, lead_diag, far_offsets, near_first, near_second, tile_counts
):
    near_total = near_cache.shape[0]
    cached, size = response_cache.shape[:2]
    share = cached * size // lax.axis_size("row")
    own = lax.dynamic_slice_in_dim(
        response_cache.reshape(cached * size, size), lax.axis_index("row") * share, share, 0
    )
    blocks = lax.all_gather(own, ("col", "row"), axis=0, tiled=True).reshape(-1, size, size)
    pairs = total_pairs(local_pairs(near_first, near_second, tile_counts, near_total))
    turned = jnp.transpose(near_cache, (0, 2, 1))
    padded = jnp.concatenate([turned, jnp.zeros_like(turned[:1])], axis=0)
    lead_factor, parts = lead(pairs, near_cache, turned, lead_diag)
    usable = jnp.arange(far_offsets.shape[1], dtype=jnp.int32)[None, :] < tile_counts[:, None]
    info = jnp.concatenate(
        [far_offsets]
        + [jnp.where(usable, labels, near_total) for labels in (near_first, near_second)]
        + [tile_counts[:, None]],
        axis=1,
    )
    far_factor = far(info, blocks, padded, parts)
    return lead_factor, far_factor


def solution(mesh):
    return jax.shard_map(
        shards,
        mesh=mesh,
        in_specs=(
            P("col", None, None),
            P(),
            P(),
            P(("row", "col"), None),
            P(("row", "col"), None),
            P(("row", "col"), None),
            P(("row", "col")),
        ),
        out_specs=(P(), P(("row", "col"), None)),
        check_vma=False,
    )
```

```python
import functools

import jax
import jax.numpy as jnp
from jax import lax
from jax.experimental import pallas as pl
from jax.experimental.pallas import tpu as pltpu
from jax.sharding import PartitionSpec as P

HIGHEST = lax.Precision.HIGHEST
BLOCK = 128
GROUP = 4
SIDE = 4
CACHED = 16
HALF = CACHED // 2
RING = 2


def dot32(left, right):
    return jnp.dot(left, right, precision=HIGHEST, preferred_element_type=jnp.float32)


def split3(value):
    high = value.astype(jnp.bfloat16)
    rest = value - high.astype(jnp.float32)
    middle = rest.astype(jnp.bfloat16)
    low = (rest - middle.astype(jnp.float32)).astype(jnp.bfloat16)
    return high, middle, low


def spread_rows(value, row):
    return jnp.broadcast_to(value[row : row + 1, :], (8, BLOCK))


def factor_block(block):
    groups = BLOCK // 8
    sub = lax.broadcasted_iota(jnp.int32, (8, BLOCK), 0)
    lane = lax.broadcasted_iota(jnp.int32, (8, BLOCK), 1)
    main = [block[8 * g : 8 * g + 8, :] for g in range(groups)]
    side = [(lane == sub + 8 * g).astype(jnp.float32) for g in range(groups)]
    for panel in range(groups):
        start = 8 * panel
        cols = {
            (g, m): jnp.broadcast_to(main[g][:, start + m : start + m + 1], (8, BLOCK))
            for g in range(panel, groups)
            for m in range(8)
        }
        scale = jnp.ones((8, BLOCK), jnp.float32)
        for j in range(8):
            pivots = {m: spread_rows(cols[panel, m], j) for m in range(j, 8)}
            root = lax.rsqrt(pivots[j])
            root = root * (1.5 - 0.5 * pivots[j] * root * root)
            inverse = root * root
            scale = jnp.where(sub == j, root, scale)
            main_row = spread_rows(main[panel], j)
            side_row = spread_rows(side[panel], j)
            for g in range(panel, groups):
                ratio = cols[g, j] * inverse
                if g == panel:
                    ratio = jnp.where(sub > j, ratio, 0.0)
                for m in range(j + 1, 8):
                    cols[g, m] = cols[g, m] - ratio * pivots[m]
                main[g] = main[g] - ratio * main_row
                side[g] = side[g] - ratio * side_row
        main[panel] = main[panel] * scale
        side[panel] = side[panel] * scale
    for g in range(groups):
        main[g] = jnp.where(lane >= sub + 8 * g, main[g], 0.0)
        side[g] = jnp.where(lane <= sub + 8 * g, side[g], 0.0)
    return jnp.concatenate(main, axis=0), jnp.concatenate(side, axis=0)


def factor_steps(work, upper, begin, end):
    whole = upper.shape[0]
    rows = lax.broadcasted_iota(jnp.int32, (BLOCK, whole), 0)
    columns = lax.broadcasted_iota(jnp.int32, (BLOCK, whole), 1)

    def step(b, carry):
        base = pl.multiple_of(b * BLOCK, BLOCK)
        own = pl.ds(base, BLOCK)
        _, turned = factor_block(work[own, own])
        solved = dot32(turned, work[own, :])
        solved_main = jnp.where(columns >= base + rows, solved[:, :whole], 0.0)
        upper[own, :] = solved_main
        work[own, whole:] = solved[:, whole:]
        below = jnp.where(columns >= base + BLOCK, solved_main, 0.0)
        change = dot32(below.T, jnp.concatenate([below, solved[:, whole:]], axis=1))
        work[...] = work[...] - change
        return carry

    lax.fori_loop(begin, end, step, 0)


def lead_start_kernel(pairs_ref, near_ref, turned_ref, diag_ref, work, upper):
    near_total, size, _ = near_ref.shape
    whole = 2 * size
    first_sums = [sum(pairs_ref[j, k] for k in range(near_total)) for j in range(near_total)]
    second_sums = [sum(pairs_ref[j, k] for j in range(near_total)) for k in range(near_total)]
    work[...] = jnp.zeros_like(work)
    for j in range(near_total):
        left = turned_ref[j]
        mixed = jnp.zeros((size, size), jnp.float32)
        for k in range(near_total):
            product = jnp.dot(left, near_ref[k], preferred_element_type=jnp.float32)
            mixed = mixed + pairs_ref[j, k] * product
            if k == j:
                own = product
        work[:size, :size] += first_sums[j] * own
        work[size:, size:whole] += second_sums[j] * own
        work[:size, size:whole] += mixed
    rows = lax.broadcasted_iota(jnp.int32, (whole, whole), 0)
    columns = lax.broadcasted_iota(jnp.int32, (whole, whole), 1)
    same = rows == columns
    work[:, :whole] += jnp.where(same, jnp.broadcast_to(diag_ref[...], (whole, whole)), 0.0)
    work[:, whole:] = same.astype(jnp.float32)
    factor_steps(work, upper, 0, size // BLOCK)


def lead_end_kernel(work_ref, upper_ref, factor_ref, parts_ref, work, upper):
    whole = upper.shape[0]
    half = whole // 2
    work[...] = work_ref[...]
    upper[:half, :] = upper_ref[:half, :]
    factor_steps(work, upper, half // BLOCK, whole // BLOCK)
    factor_ref[...] = upper[...].T
    for n, part in enumerate(split3(work[:, whole:].T)):
        for i in range(2):
            for j in range(2):
                parts_ref[n, i, j] = part[i * half : (i + 1) * half, j * half : (j + 1) * half]


VMEM = pl.BlockSpec(memory_space=pltpu.VMEM)


def lead_start(pairs, near_cache, turned_near, lead_diag):
    whole = lead_diag.shape[0]
    return pl.pallas_call(
        lead_start_kernel,
        out_shape=(
            jax.ShapeDtypeStruct((whole, 2 * whole), jnp.float32),
            jax.ShapeDtypeStruct((whole, whole), jnp.float32),
        ),
        in_specs=[pl.BlockSpec(memory_space=pltpu.SMEM), VMEM, VMEM, VMEM],
        out_specs=(VMEM, VMEM),
        compiler_params=pltpu.CompilerParams(vmem_limit_bytes=24 << 20),
        cost_estimate=pl.CostEstimate(
            flops=9_000_000_000, bytes_accessed=6 << 20, transcendentals=0
        ),
        name="lead_start",
    )(pairs, near_cache, turned_near, lead_diag.reshape(1, whole))


def lead_end(work, upper):
    whole = upper.shape[0]
    square = jax.ShapeDtypeStruct((whole, whole), jnp.float32)
    return pl.pallas_call(
        lead_end_kernel,
        out_shape=(square, jax.ShapeDtypeStruct((3, 2, 2, whole // 2, whole // 2), jnp.bfloat16)),
        in_specs=[VMEM, VMEM],
        out_specs=(VMEM, VMEM),
        scratch_shapes=[
            pltpu.VMEM((whole, 2 * whole), jnp.float32),
            pltpu.VMEM((whole, whole), jnp.float32),
        ],
        compiler_params=pltpu.CompilerParams(vmem_limit_bytes=24 << 20),
        cost_estimate=pl.CostEstimate(
            flops=9_000_000_000, bytes_accessed=6 << 20, transcendentals=0
        ),
        name="lead_end",
    )(work, upper)


def ring_places(offsets, core, y, z):
    col, local = offsets // CACHED, offsets % CACHED
    half, inner = local // HALF, local % HALF
    sign = 1 - 2 * core
    from_y = (sign * (y - col // SIDE)) & (SIDE - 1)
    from_z = (sign * (z - col % SIDE)) & (SIDE - 1)
    by_z = inner < RING
    major = jnp.where(by_z, from_z, from_y)
    minor = jnp.where(by_z, from_y, from_z)
    place = jnp.where(by_z, inner, inner - RING + SIDE * SIDE * RING)
    held = (half == core) & (inner < 2 * RING)
    return jnp.where(held, (major * SIDE + minor) * RING + place, -1)


def spread_places(offsets):
    col, local = offsets // CACHED, offsets % CACHED
    half, inner = local // HALF, local % HALF
    kept = HALF - 2 * RING
    place = col * (2 * kept) + half * kept + inner - 2 * RING
    return jnp.where(inner >= 2 * RING, place, -1)


def list_slots(tile, info_ref, items, slots):
    def visit(s, count):
        place = info_ref[tile, s]
        items[0, tile, count] = place
        items[1, tile, count] = info_ref[tile, slots + s]
        items[2, tile, count] = info_ref[tile, 2 * slots + s]
        return count + (place >= 0).astype(jnp.int32)

    return lax.fori_loop(0, slots, visit, 0)


def left_rows(tile, r, count, items, turned_ref):
    empty = turned_ref.shape[0] - 1
    firsts, seconds = [], []
    for i in range(GROUP):
        q = r * GROUP + i
        used = q < count
        firsts.append(turned_ref[jnp.where(used, items[1, tile, q], empty)])
        seconds.append(turned_ref[jnp.where(used, items[2, tile, q], empty)])
    return jnp.concatenate(
        [jnp.concatenate(firsts, axis=1), jnp.concatenate(seconds, axis=1)], axis=0
    )


def ring_kernel(slots, info_ref, turned_ref, *refs):
    *pieces, out_ref, held, items, arrived = refs
    size = turned_ref.shape[1]
    tile = pl.program_id(0)
    copies = []
    start = 0
    for n, piece in enumerate(pieces):
        copies.append(
            pltpu.make_async_copy(piece, held.at[pl.ds(start, piece.shape[0])], arrived.at[n])
        )
        start += piece.shape[0]

    @pl.when(tile == 0)
    def fetch():
        for copy in copies:
            copy.start()

    count = list_slots(tile, info_ref, items, slots)

    @pl.when(tile == 0)
    def wait():
        for copy in copies:
            copy.wait()

    out_ref[...] = jnp.zeros_like(out_ref)

    def one_round(r, carry):
        rights = []
        for i in range(GROUP):
            q = r * GROUP + i
            rights.append(held[jnp.where(q < count, items[0, tile, q], 0)])
        out_ref[0] += jnp.dot(
            left_rows(tile, r, count, items, turned_ref),
            jnp.concatenate(rights, axis=0),
            preferred_element_type=jnp.float32,
        )
        return carry

    lax.fori_loop(0, (count + GROUP - 1) // GROUP, one_round, 0)


def ring_sums(info, slots, turned_near, pieces):
    tiles = info.shape[0]
    size = turned_near.shape[1]
    per_tile = pl.BlockSpec((1, 2 * size, size), lambda t, *_: (t, 0, 0))
    return pl.pallas_call(
        functools.partial(ring_kernel, slots),
        out_shape=jax.ShapeDtypeStruct((tiles, 2 * size, size), jnp.float32),
        grid_spec=pltpu.PrefetchScalarGridSpec(
            num_scalar_prefetch=1,
            grid=(tiles,),
            in_specs=[pl.BlockSpec(turned_near.shape, lambda t, *_: (0, 0, 0))]
            + [pl.BlockSpec(memory_space=pltpu.HBM)] * len(pieces),
            out_specs=per_tile,
            scratch_shapes=[
                pltpu.VMEM((sum(p.shape[0] for p in pieces), size, size), jnp.bfloat16),
                pltpu.SMEM((3, tiles, slots), jnp.int32),
                pltpu.SemaphoreType.DMA((len(pieces),)),
            ],
        ),
        compiler_params=pltpu.CompilerParams(
            dimension_semantics=("arbitrary",), vmem_limit_bytes=60 << 20
        ),
        cost_estimate=pl.CostEstimate(
            flops=3_000_000_000, bytes_accessed=12 << 20, transcendentals=0
        ),
        name="ring_sums",
    )(info, turned_near, *pieces)


def far_kernel(
    slots, sums, info_ref, own_hbm, other_hbm, blocks_ref, turned_hbm, parts_hbm, out_hbm, held,
    own_ref, other_ref, turned_ref, parts_ref, out_ref, items, counts, arrived, loaded, stored,
):
    tiles = info_ref.shape[0]
    size = turned_ref.shape[1]
    empty = turned_ref.shape[0] - 1

    def rounds_of(t):
        return (counts[t] + GROUP - 1) // GROUP

    def begin(t, r):
        for i in range(GROUP):
            s = r * GROUP + i
            place = jnp.where(s < counts[t], items[0, t, s], 0)
            pltpu.make_async_copy(
                blocks_ref.at[place], held.at[t, s], arrived.at[t, r]
            ).start()

    def begin_rounds(t, first, past):
        def begin_round(r, carry):
            begin(t, r)
            return carry

        lax.fori_loop(first, past, begin_round, 0)

    def finish(t, r):
        pltpu.make_async_copy(
            blocks_ref.at[pl.ds(0, GROUP)],
            held.at[t, pl.ds(r * GROUP, GROUP)],
            arrived.at[t, r],
        ).wait()

    def store(t):
        rows = pl.ds(pl.multiple_of(t * size, size), size)
        return pltpu.make_async_copy(out_ref.at[t], out_hbm.at[rows, :], stored.at[t])

    def multiply(total, unit, terms):
        for n, (left, right) in enumerate(terms):
            pltpu.matmul_push_rhs(right, n % 2, unit)
            pltpu.matmul_acc_lhs(total, left, n % 2)

    def main(first_sum, second_sum):
        load_turned = pltpu.make_async_copy(turned_hbm, turned_ref, loaded.at[0])
        load_parts = pltpu.make_async_copy(parts_hbm, parts_ref, loaded.at[1])
        load_own = pltpu.make_async_copy(own_hbm, own_ref, loaded.at[2])
        load_other = pltpu.make_async_copy(other_hbm, other_ref, loaded.at[3])
        load_turned.start()
        for t in range(tiles):
            counts[t] = list_slots(t, info_ref, items, slots)
            if t == 0:
                begin_rounds(0, 0, rounds_of(0))
        load_parts.start()
        load_own.start()
        load_other.start()
        pltpu.matmul_pop(first_sum)
        pltpu.matmul_pop(second_sum)
        load_turned.wait()

        def tile_step(t, carry):
            rounds = rounds_of(t)
            following = jnp.minimum(t + 1, tiles - 1)
            next_rounds = jnp.where(t + 1 < tiles, rounds_of(following), 0)

            def one_round(r, carry):
                @pl.when(r < next_rounds)
                def fetch():
                    begin(following, r)

                finish(t, r)
                for i in range(GROUP):
                    s = r * GROUP + i
                    used = s < counts[t]
                    block = held[t, s]
                    pltpu.matmul_push_rhs(block, i % 2, 0)
                    pltpu.matmul_push_rhs(block, i % 2, 1)
                    first = jnp.where(used, items[1, t, s], empty)
                    second = jnp.where(used, items[2, t, s], empty)
                    pltpu.matmul_acc_lhs(first_sum, turned_ref[first], i % 2)
                    pltpu.matmul_acc_lhs(second_sum, turned_ref[second], i % 2)
                return carry

            lax.fori_loop(0, rounds, one_round, 0)
            begin_rounds(following, rounds, jnp.maximum(rounds, next_rounds))

            @pl.when(t == 0)
            def factors():
                load_parts.wait()
                load_own.wait()
                load_other.wait()

            before = own_ref[t] + other_ref[t]
            rows = (
                split3((pltpu.matmul_pop(first_sum) + before[:size]).T),
                split3((pltpu.matmul_pop(second_sum) + before[size:]).T),
            )
            products = ((0, 0), (0, 1), (1, 0), (0, 2), (1, 1), (2, 0))

            def terms(half, columns, chosen):
                return [(rows[half][i], parts_ref[j, half, columns]) for i, j in chosen]

            multiply(first_sum, 0, terms(0, 0, products))
            multiply(second_sum, 1, terms(0, 1, products) + terms(1, 1, products[3:]))
            out_ref[t, :, :size] = pltpu.matmul_pop(first_sum)
            multiply(first_sum, 0, terms(1, 1, products[:3]))
            out_ref[t, :, size:] = pltpu.matmul_pop(second_sum) + pltpu.matmul_pop(first_sum)
            store(t).start()
            return carry

        lax.fori_loop(0, tiles, tile_step, 0)
        for t in range(tiles):
            store(t).wait()

    pl.run_scoped(main, *sums)


def far(info, slots, own_sums, other_sums, blocks, turned_near, parts):
    tiles = info.shape[0]
    size = blocks.shape[1]
    hbm = pl.BlockSpec(memory_space=pltpu.HBM)
    sums = [pltpu.ACC(mxu_id=n)((size, size), jnp.float32) for n in range(2)]
    return pl.pallas_call(
        functools.partial(far_kernel, slots, sums),
        out_shape=jax.ShapeDtypeStruct((tiles * size, 2 * size), jnp.float32),
        in_specs=[pl.BlockSpec(memory_space=pltpu.SMEM)] + [hbm] * 5,
        out_specs=hbm,
        scratch_shapes=[
            pltpu.VMEM((tiles, slots, size, size), jnp.bfloat16),
            pltpu.VMEM(own_sums.shape, jnp.float32),
            pltpu.VMEM(own_sums.shape, jnp.float32),
            pltpu.VMEM(turned_near.shape, jnp.bfloat16),
            pltpu.VMEM(parts.shape, jnp.bfloat16),
            pltpu.VMEM((tiles, size, 2 * size), jnp.float32),
            pltpu.SMEM((3, tiles, slots + 1), jnp.int32),
            pltpu.SMEM((tiles,), jnp.int32),
            pltpu.SemaphoreType.DMA((tiles, slots // GROUP)),
            pltpu.SemaphoreType.DMA((4,)),
            pltpu.SemaphoreType.DMA((tiles,)),
        ],
        compiler_params=pltpu.CompilerParams(vmem_limit_bytes=63 << 20),
        name="far",
    )(info, own_sums, other_sums, blocks, turned_near, parts)


def local_pairs(near_first, near_second, counts, near_total):
    slots = near_first.shape[1]
    usable = jnp.arange(slots, dtype=jnp.int32)[None, :] < counts[:, None]
    labels = jnp.arange(near_total, dtype=jnp.int32)
    first_hot = (near_first[:, :, None] == labels) & usable[:, :, None]
    second_hot = near_second[:, :, None] == labels
    both = first_hot[:, :, :, None] & second_hot[:, :, None, :]
    return jnp.sum(both.astype(jnp.float32), axis=(0, 1))


def hop(value, along_y):
    rows, cols = lax.axis_size("row"), lax.axis_size("col")
    moves = []
    for row in range(rows):
        sign = 1 - 2 * (row % 2)
        for col in range(cols):
            y, z = col // SIDE, col % SIDE
            y, z = ((y + sign) % SIDE, z) if along_y else (y, (z + sign) % SIDE)
            moves.append((row * cols + col, row * cols + y * SIDE + z))
    return lax.ppermute(value, ("row", "col"), moves)


def swap(value, axis, bit):
    return lax.ppermute(value, axis, [(i, i ^ bit) for i in range(lax.axis_size(axis))])


def shards(
    response_cache, near_cache, lead_diag, far_offsets, near_first, near_second, tile_counts
):
    near_total = near_cache.shape[0]
    slots = far_offsets.shape[1]
    row = lax.axis_index("row")
    core = row % 2
    kept = HALF - 2 * RING
    share = 2 * kept // lax.axis_size("row")
    at = row * share
    own = lax.dynamic_slice_in_dim(
        response_cache, at // kept * HALF + 2 * RING + at % kept, share, 0
    )
    blocks = lax.all_gather(own, ("col", "row"), axis=0, tiled=True)
    line_y = [lax.dynamic_slice_in_dim(response_cache, core * HALF, RING, 0)]
    line_z = [lax.dynamic_slice_in_dim(response_cache, core * HALF + RING, RING, 0)]
    usable = jnp.arange(slots, dtype=jnp.int32)[None, :] < tile_counts[:, None]
    y, z = lax.axis_index("col") // SIDE, lax.axis_index("col") % SIDE
    info, info_own, info_other = (
        jnp.concatenate([jnp.where(usable, places, -1), near_first, near_second], axis=1)
        for places in (
            spread_places(far_offsets),
            ring_places(far_offsets, core, y, z),
            ring_places(far_offsets, 1 - core, y, z),
        )
    )
    turned = jnp.transpose(near_cache, (0, 2, 1))
    padded = jnp.concatenate([turned, jnp.zeros_like(turned[:1])], axis=0)
    pairs = local_pairs(near_first, near_second, tile_counts, near_total)

    def advance(pairs, rings, stages):
        (to_z, along_y), (to_y, along_z) = rings
        to_z, to_y = hop(to_z, along_y), hop(to_y, along_z)
        for axis, bit in stages:
            pairs = pairs + swap(pairs, axis, bit)
        return lax.optimization_barrier((pairs, to_z, to_y))

    for stages in ((("col", 8),), (("col", 4), ("col", 2)), (("col", 1),)):
        pairs, step_y, step_z = advance(
            pairs, ((line_y[-1], True), (line_z[-1], False)), stages
        )
        line_y.append(step_y)
        line_z.append(step_z)
    by_z = [jnp.concatenate(line_y, axis=0)]
    by_y = [jnp.concatenate(line_z, axis=0)]
    pairs, step_z, step_y = advance(
        pairs, ((by_z[-1], False), (by_y[-1], True)), (("row", 1), ("row", 4), ("row", 2))
    )
    by_z.append(step_z)
    by_y.append(step_y)
    step_z, step_y = hop(by_z[-1], False), hop(by_y[-1], True)
    info_other = swap(info_other, "row", 1)
    pairs, info_other = lax.optimization_barrier((pairs, info_other))
    work, upper = lead_start(pairs, near_cache, turned, lead_diag)
    work, step_z, step_y = lax.optimization_barrier((work, step_z, step_y))
    by_z.append(step_z)
    by_y.append(step_y)
    step_z, step_y = hop(by_z[-1], False), hop(by_y[-1], True)
    lead_factor, parts = lead_end(work, upper)
    parts, step_z, step_y = lax.optimization_barrier((parts, step_z, step_y))
    pieces = by_z + [step_z] + by_y + [step_y]
    sums_other = ring_sums(info_other, slots, padded, pieces)
    moved = swap(sums_other, "row", 1)
    sums = ring_sums(info_own, slots, padded, pieces)
    far_factor = far(info, slots, sums, moved, blocks, padded, parts)
    return lead_factor, far_factor


def solution(mesh):
    return jax.shard_map(
        shards,
        mesh=mesh,
        in_specs=(
            P("col", None, None),
            P(),
            P(),
            P(("row", "col"), None),
            P(("row", "col"), None),
            P(("row", "col"), None),
            P(("row", "col")),
        ),
        out_specs=(P(), P(("row", "col"), None)),
        check_vma=False,
    )
```

```python
import functools

import jax
import jax.numpy as jnp
from jax import lax
from jax.experimental import pallas as pl
from jax.experimental.pallas import tpu as pltpu
from jax.sharding import PartitionSpec as P

HIGHEST = lax.Precision.HIGHEST
BLOCK = 128
GROUP = 4


def dot32(left, right):
    return jnp.dot(left, right, precision=HIGHEST, preferred_element_type=jnp.float32)


def split3(value):
    high = value.astype(jnp.bfloat16)
    rest = value - high.astype(jnp.float32)
    middle = rest.astype(jnp.bfloat16)
    low = (rest - middle.astype(jnp.float32)).astype(jnp.bfloat16)
    return high, middle, low


def spread_rows(value, row):
    return jnp.broadcast_to(value[row : row + 1, :], (8, BLOCK))


def factor_block(block):
    groups = BLOCK // 8
    sub = lax.broadcasted_iota(jnp.int32, (8, BLOCK), 0)
    lane = lax.broadcasted_iota(jnp.int32, (8, BLOCK), 1)
    main = [block[8 * g : 8 * g + 8, :] for g in range(groups)]
    side = [(lane == sub + 8 * g).astype(jnp.float32) for g in range(groups)]
    for panel in range(groups):
        start = 8 * panel
        cols = {
            (g, m): jnp.broadcast_to(main[g][:, start + m : start + m + 1], (8, BLOCK))
            for g in range(panel, groups)
            for m in range(8)
        }
        scale = jnp.ones((8, BLOCK), jnp.float32)
        for j in range(8):
            pivots = {m: spread_rows(cols[panel, m], j) for m in range(j, 8)}
            root = lax.rsqrt(pivots[j])
            root = root * (1.5 - 0.5 * pivots[j] * root * root)
            inverse = root * root
            scale = jnp.where(sub == j, root, scale)
            main_row = spread_rows(main[panel], j)
            side_row = spread_rows(side[panel], j)
            for g in range(panel, groups):
                ratio = cols[g, j] * inverse
                if g == panel:
                    ratio = jnp.where(sub > j, ratio, 0.0)
                for m in range(j + 1, 8):
                    cols[g, m] = cols[g, m] - ratio * pivots[m]
                main[g] = main[g] - ratio * main_row
                side[g] = side[g] - ratio * side_row
        main[panel] = main[panel] * scale
        side[panel] = side[panel] * scale
    for g in range(groups):
        main[g] = jnp.where(lane >= sub + 8 * g, main[g], 0.0)
        side[g] = jnp.where(lane <= sub + 8 * g, side[g], 0.0)
    return jnp.concatenate(main, axis=0), jnp.concatenate(side, axis=0)


def lead_kernel(pairs_ref, near_ref, turned_ref, diag_ref, factor_ref, parts_ref, work, upper):
    near_total, size, _ = near_ref.shape
    whole = 2 * size
    first_sums = [sum(pairs_ref[j, k] for k in range(near_total)) for j in range(near_total)]
    second_sums = [sum(pairs_ref[j, k] for j in range(near_total)) for k in range(near_total)]
    work[...] = jnp.zeros_like(work)
    for j in range(near_total):
        left = turned_ref[j]
        mixed = jnp.zeros((size, size), jnp.float32)
        for k in range(near_total):
            product = jnp.dot(left, near_ref[k], preferred_element_type=jnp.float32)
            mixed = mixed + pairs_ref[j, k] * product
            if k == j:
                own = product
        work[:size, :size] += first_sums[j] * own
        work[size:, size:whole] += second_sums[j] * own
        work[:size, size:whole] += mixed
    rows = lax.broadcasted_iota(jnp.int32, (whole, whole), 0)
    columns = lax.broadcasted_iota(jnp.int32, (whole, whole), 1)
    same = rows == columns
    work[:, :whole] += jnp.where(same, jnp.broadcast_to(diag_ref[...], (whole, whole)), 0.0)
    work[:, whole:] = same.astype(jnp.float32)

    def step(b, carry):
        base = pl.multiple_of(b * BLOCK, BLOCK)
        own = pl.ds(base, BLOCK)
        _, turned = factor_block(work[own, own])
        solved = dot32(turned, work[own, :])
        at = columns[:BLOCK, :] >= base + rows[:BLOCK, :]
        solved_main = jnp.where(at, solved[:, :whole], 0.0)
        upper[own, :] = solved_main
        work[own, whole:] = solved[:, whole:]
        below = jnp.where(columns[:BLOCK, :] >= base + BLOCK, solved_main, 0.0)
        change = dot32(below.T, jnp.concatenate([below, solved[:, whole:]], axis=1))
        work[...] = work[...] - change
        return carry

    lax.fori_loop(0, whole // BLOCK, step, 0)
    factor_ref[...] = upper[...].T
    high, middle, low = split3(work[:, whole:].T)
    for n, part in enumerate((high, middle, low)):
        for half in range(2):
            for columns in range(2):
                parts_ref[n, half, columns] = part[
                    half * size : (half + 1) * size, columns * size : (columns + 1) * size
                ]


def lead(pairs, near_cache, turned_near, lead_diag):
    whole = lead_diag.shape[0]
    vmem = pl.BlockSpec(memory_space=pltpu.VMEM)
    return pl.pallas_call(
        lead_kernel,
        out_shape=(
            jax.ShapeDtypeStruct((whole, whole), jnp.float32),
            jax.ShapeDtypeStruct((3, 2, 2, whole // 2, whole // 2), jnp.bfloat16),
        ),
        in_specs=[pl.BlockSpec(memory_space=pltpu.SMEM), vmem, vmem, vmem],
        out_specs=(vmem, vmem),
        scratch_shapes=[
            pltpu.VMEM((whole, 2 * whole), jnp.float32),
            pltpu.VMEM((whole, whole), jnp.float32),
        ],
        compiler_params=pltpu.CompilerParams(vmem_limit_bytes=40 << 20),
        name="lead",
    )(pairs, near_cache, turned_near, lead_diag.reshape(1, whole))


def far_kernel(
    slots, sums, info_ref, blocks_ref, turned_hbm, parts_hbm, out_hbm, held, turned_ref, parts_ref,
    out_ref, arrived, loaded, stored,
):
    tiles = info_ref.shape[0]
    size = turned_ref.shape[1]

    def rounds_of(t):
        return (info_ref[t, 3 * slots] + GROUP - 1) // GROUP

    def begin(t, r):
        for i in range(GROUP):
            s = r * GROUP + i
            pltpu.make_async_copy(
                blocks_ref.at[info_ref[t, s]], held.at[t, s], arrived.at[t, r]
            ).start()

    def begin_rounds(t, first, past):
        def begin_round(r, carry):
            begin(t, r)
            return carry

        lax.fori_loop(first, past, begin_round, 0)

    def finish(t, r):
        pltpu.make_async_copy(
            blocks_ref.at[pl.ds(0, GROUP)],
            held.at[t, pl.ds(r * GROUP, GROUP)],
            arrived.at[t, r],
        ).wait()

    def store(t):
        rows = pl.ds(pl.multiple_of(t * size, size), size)
        return pltpu.make_async_copy(out_ref.at[t], out_hbm.at[rows, :], stored.at[t])

    def multiply(total, unit, terms):
        for n, (left, right) in enumerate(terms):
            pltpu.matmul_push_rhs(right, n % 2, unit)
            pltpu.matmul_acc_lhs(total, left, n % 2)

    def main(first_sum, second_sum):
        load_turned = pltpu.make_async_copy(turned_hbm, turned_ref, loaded.at[0])
        load_parts = pltpu.make_async_copy(parts_hbm, parts_ref, loaded.at[1])
        load_turned.start()
        begin_rounds(0, 0, rounds_of(0))
        load_parts.start()
        pltpu.matmul_pop(first_sum)
        pltpu.matmul_pop(second_sum)
        load_turned.wait()

        def tile_step(t, carry):
            rounds = rounds_of(t)
            following = jnp.minimum(t + 1, tiles - 1)
            next_rounds = jnp.where(t + 1 < tiles, rounds_of(following), 0)

            def one_round(r, carry):
                @pl.when(r < next_rounds)
                def fetch():
                    begin(following, r)

                finish(t, r)
                for i in range(GROUP):
                    s = r * GROUP + i
                    block = held[t, s]
                    pltpu.matmul_push_rhs(block, i % 2, 0)
                    pltpu.matmul_push_rhs(block, i % 2, 1)
                    pltpu.matmul_acc_lhs(first_sum, turned_ref[info_ref[t, slots + s]], i % 2)
                    pltpu.matmul_acc_lhs(second_sum, turned_ref[info_ref[t, 2 * slots + s]], i % 2)
                return carry

            lax.fori_loop(0, rounds, one_round, 0)
            begin_rounds(following, rounds, jnp.maximum(rounds, next_rounds))

            @pl.when(t == 0)
            def factors():
                load_parts.wait()

            rows = (
                split3(pltpu.matmul_pop(first_sum).T),
                split3(pltpu.matmul_pop(second_sum).T),
            )
            products = ((0, 0), (0, 1), (1, 0), (0, 2), (1, 1), (2, 0))

            def terms(half, columns, chosen):
                return [(rows[half][i], parts_ref[j, half, columns]) for i, j in chosen]

            multiply(first_sum, 0, terms(0, 0, products))
            multiply(second_sum, 1, terms(0, 1, products) + terms(1, 1, products[3:]))
            out_ref[t, :, :size] = pltpu.matmul_pop(first_sum)
            multiply(first_sum, 0, terms(1, 1, products[:3]))
            out_ref[t, :, size:] = pltpu.matmul_pop(second_sum) + pltpu.matmul_pop(first_sum)
            store(t).start()
            return carry

        lax.fori_loop(0, tiles, tile_step, 0)
        for t in range(tiles):
            store(t).wait()

    pl.run_scoped(main, *sums)


def far(info, blocks, turned_near, parts):
    tiles = info.shape[0]
    slots = info.shape[1] // 3
    size = blocks.shape[1]
    hbm = pl.BlockSpec(memory_space=pltpu.HBM)
    sums = [pltpu.ACC(mxu_id=n)((size, size), jnp.float32) for n in range(2)]
    return pl.pallas_call(
        functools.partial(far_kernel, slots, sums),
        out_shape=jax.ShapeDtypeStruct((tiles * size, 2 * size), jnp.float32),
        in_specs=[pl.BlockSpec(memory_space=pltpu.SMEM), hbm, hbm, hbm],
        out_specs=hbm,
        scratch_shapes=[
            pltpu.VMEM((tiles, slots, size, size), jnp.bfloat16),
            pltpu.VMEM(turned_near.shape, jnp.bfloat16),
            pltpu.VMEM(parts.shape, jnp.bfloat16),
            pltpu.VMEM((tiles, size, 2 * size), jnp.float32),
            pltpu.SemaphoreType.DMA((tiles, slots // GROUP)),
            pltpu.SemaphoreType.DMA((2,)),
            pltpu.SemaphoreType.DMA((tiles,)),
        ],
        compiler_params=pltpu.CompilerParams(vmem_limit_bytes=63 << 20),
        name="far",
    )(info, blocks, turned_near, parts)


def local_pairs(near_first, near_second, counts, near_total):
    slots = near_first.shape[1]
    usable = jnp.arange(slots, dtype=jnp.int32)[None, :] < counts[:, None]
    labels = jnp.arange(near_total, dtype=jnp.int32)
    first_hot = (near_first[:, :, None] == labels) & usable[:, :, None]
    second_hot = near_second[:, :, None] == labels
    both = first_hot[:, :, :, None] & second_hot[:, :, None, :]
    return jnp.sum(both.astype(jnp.float32), axis=(0, 1))


def total_pairs(value):
    for axis, bits in (("row", (1, 4, 2)), ("col", (8, 4, 2, 1))):
        size = lax.axis_size(axis)
        for bit in bits:
            value = value + lax.ppermute(value, axis, [(i, i ^ bit) for i in range(size)])
    return value


def shards(
    response_cache, near_cache, lead_diag, far_offsets, near_first, near_second, tile_counts
):
    near_total = near_cache.shape[0]
    share = response_cache.shape[0] // lax.axis_size("row")
    own = lax.dynamic_slice_in_dim(response_cache, lax.axis_index("row") * share, share, 0)
    blocks = lax.all_gather(own, ("col", "row"), axis=0, tiled=True)
    turned = jnp.transpose(near_cache, (0, 2, 1))
    padded = jnp.concatenate([turned, jnp.zeros_like(turned[:1])], axis=0)
    labels, turned, padded = lax.optimization_barrier((near_first, turned, padded))
    pairs = total_pairs(local_pairs(labels, near_second, tile_counts, near_total))
    lead_factor, parts = lead(pairs, near_cache, turned, lead_diag)
    usable = jnp.arange(far_offsets.shape[1], dtype=jnp.int32)[None, :] < tile_counts[:, None]
    info = jnp.concatenate(
        [far_offsets]
        + [jnp.where(usable, chosen, near_total) for chosen in (near_first, near_second)]
        + [tile_counts[:, None]],
        axis=1,
    )
    far_factor = far(info, blocks, padded, parts)
    return lead_factor, far_factor


def solution(mesh):
    return jax.shard_map(
        shards,
        mesh=mesh,
        in_specs=(
            P("col", None, None),
            P(),
            P(),
            P(("row", "col"), None),
            P(("row", "col"), None),
            P(("row", "col"), None),
            P(("row", "col")),
        ),
        out_specs=(P(), P(("row", "col"), None)),
        check_vma=False,
    )
```

```python
import functools

import jax
import jax.numpy as jnp
from jax import lax
from jax.experimental import pallas as pl
from jax.experimental.pallas import tpu as pltpu
from jax.sharding import PartitionSpec as P

HIGHEST = lax.Precision.HIGHEST
BLOCK = 128
GROUP = 4


def dot32(left, right):
    return jnp.dot(left, right, precision=HIGHEST, preferred_element_type=jnp.float32)


def split3(value):
    high = value.astype(jnp.bfloat16)
    rest = value - high.astype(jnp.float32)
    middle = rest.astype(jnp.bfloat16)
    low = (rest - middle.astype(jnp.float32)).astype(jnp.bfloat16)
    return high, middle, low


def spread_rows(value, row):
    return jnp.broadcast_to(value[row : row + 1, :], (8, BLOCK))


def factor_block(block):
    groups = BLOCK // 8
    sub = lax.broadcasted_iota(jnp.int32, (8, BLOCK), 0)
    lane = lax.broadcasted_iota(jnp.int32, (8, BLOCK), 1)
    main = [block[8 * g : 8 * g + 8, :] for g in range(groups)]
    side = [(lane == sub + 8 * g).astype(jnp.float32) for g in range(groups)]
    for panel in range(groups):
        start = 8 * panel
        cols = {
            (g, m): jnp.broadcast_to(main[g][:, start + m : start + m + 1], (8, BLOCK))
            for g in range(panel, groups)
            for m in range(8)
        }
        scale = jnp.ones((8, BLOCK), jnp.float32)
        for j in range(8):
            pivots = {m: spread_rows(cols[panel, m], j) for m in range(j, 8)}
            root = lax.rsqrt(pivots[j])
            root = root * (1.5 - 0.5 * pivots[j] * root * root)
            inverse = root * root
            scale = jnp.where(sub == j, root, scale)
            main_row = spread_rows(main[panel], j)
            side_row = spread_rows(side[panel], j)
            for g in range(panel, groups):
                ratio = cols[g, j] * inverse
                if g == panel:
                    ratio = jnp.where(sub > j, ratio, 0.0)
                for m in range(j + 1, 8):
                    cols[g, m] = cols[g, m] - ratio * pivots[m]
                main[g] = main[g] - ratio * main_row
                side[g] = side[g] - ratio * side_row
        main[panel] = main[panel] * scale
        side[panel] = side[panel] * scale
    for g in range(groups):
        main[g] = jnp.where(lane >= sub + 8 * g, main[g], 0.0)
        side[g] = jnp.where(lane <= sub + 8 * g, side[g], 0.0)
    return jnp.concatenate(main, axis=0), jnp.concatenate(side, axis=0)


def lead_kernel(pairs_ref, near_ref, turned_ref, diag_ref, factor_ref, parts_ref, work, upper):
    near_total, size, _ = near_ref.shape
    whole = 2 * size
    first_sums = [sum(pairs_ref[j, k] for k in range(near_total)) for j in range(near_total)]
    second_sums = [sum(pairs_ref[j, k] for j in range(near_total)) for k in range(near_total)]
    work[...] = jnp.zeros_like(work)
    for j in range(near_total):
        left = turned_ref[j]
        mixed = jnp.zeros((size, size), jnp.float32)
        for k in range(near_total):
            product = jnp.dot(left, near_ref[k], preferred_element_type=jnp.float32)
            mixed = mixed + pairs_ref[j, k] * product
            if k == j:
                own = product
        work[:size, :size] += first_sums[j] * own
        work[size:, size:whole] += second_sums[j] * own
        work[:size, size:whole] += mixed
    rows = lax.broadcasted_iota(jnp.int32, (whole, whole), 0)
    columns = lax.broadcasted_iota(jnp.int32, (whole, whole), 1)
    same = rows == columns
    work[:, :whole] += jnp.where(same, jnp.broadcast_to(diag_ref[...], (whole, whole)), 0.0)
    work[:, whole:] = same.astype(jnp.float32)

    def step(b, carry):
        base = pl.multiple_of(b * BLOCK, BLOCK)
        own = pl.ds(base, BLOCK)
        _, turned = factor_block(work[own, own])
        solved = dot32(turned, work[own, :])
        at = columns[:BLOCK, :] >= base + rows[:BLOCK, :]
        solved_main = jnp.where(at, solved[:, :whole], 0.0)
        upper[own, :] = solved_main
        work[own, whole:] = solved[:, whole:]
        below = jnp.where(columns[:BLOCK, :] >= base + BLOCK, solved_main, 0.0)
        change = dot32(below.T, jnp.concatenate([below, solved[:, whole:]], axis=1))
        work[...] = work[...] - change
        return carry

    lax.fori_loop(0, whole // BLOCK, step, 0)
    factor_ref[...] = upper[...].T
    high, middle, low = split3(work[:, whole:].T)
    for n, part in enumerate((high, middle, low)):
        for half in range(2):
            for columns in range(2):
                parts_ref[n, half, columns] = part[
                    half * size : (half + 1) * size, columns * size : (columns + 1) * size
                ]


def lead(pairs, near_cache, turned_near, lead_diag):
    whole = lead_diag.shape[0]
    vmem = pl.BlockSpec(memory_space=pltpu.VMEM)
    return pl.pallas_call(
        lead_kernel,
        out_shape=(
            jax.ShapeDtypeStruct((whole, whole), jnp.float32),
            jax.ShapeDtypeStruct((3, 2, 2, whole // 2, whole // 2), jnp.bfloat16),
        ),
        in_specs=[pl.BlockSpec(memory_space=pltpu.SMEM), vmem, vmem, vmem],
        out_specs=(vmem, vmem),
        scratch_shapes=[
            pltpu.VMEM((whole, 2 * whole), jnp.float32),
            pltpu.VMEM((whole, whole), jnp.float32),
        ],
        compiler_params=pltpu.CompilerParams(vmem_limit_bytes=40 << 20),
        name="lead",
    )(pairs, near_cache, turned_near, lead_diag.reshape(1, whole))


def far_kernel(
    slots, sums, info_ref, blocks_ref, turned_hbm, parts_hbm, out_hbm, held, turned_ref, parts_ref,
    out_ref, arrived, loaded, stored,
):
    tiles = info_ref.shape[0]
    size = turned_ref.shape[1]

    def rounds_of(t):
        return (info_ref[t, 3 * slots] + GROUP - 1) // GROUP

    def begin(t, r):
        for i in range(GROUP):
            s = r * GROUP + i
            pltpu.make_async_copy(
                blocks_ref.at[info_ref[t, s]], held.at[t, s], arrived.at[t, r]
            ).start()

    def begin_rounds(t, first, past):
        def begin_round(r, carry):
            begin(t, r)
            return carry

        lax.fori_loop(first, past, begin_round, 0)

    def finish(t, r):
        pltpu.make_async_copy(
            blocks_ref.at[pl.ds(0, GROUP)],
            held.at[t, pl.ds(r * GROUP, GROUP)],
            arrived.at[t, r],
        ).wait()

    def store(t, half):
        rows = pl.ds(pl.multiple_of(t * size, size), size)
        columns = pl.ds(half * size, size)
        return pltpu.make_async_copy(
            out_ref.at[t, half], out_hbm.at[rows, columns], stored.at[t, half]
        )

    def multiply(total, unit, terms):
        for n, (left, right) in enumerate(terms):
            pltpu.matmul_push_rhs(right, n % 2, unit)
            pltpu.matmul_acc_lhs(total, left, n % 2)

    def main(first_sum, second_sum):
        load_turned = pltpu.make_async_copy(turned_hbm, turned_ref, loaded.at[0])
        load_parts = pltpu.make_async_copy(parts_hbm, parts_ref, loaded.at[1])
        load_turned.start()
        begin_rounds(0, 0, rounds_of(0))
        load_parts.start()
        pltpu.matmul_pop(first_sum)
        pltpu.matmul_pop(second_sum)
        load_turned.wait()

        def tile_step(t, carry):
            rounds = rounds_of(t)
            following = jnp.minimum(t + 1, tiles - 1)
            next_rounds = jnp.where(t + 1 < tiles, rounds_of(following), 0)

            def one_round(r, carry):
                @pl.when(r < next_rounds)
                def fetch():
                    begin(following, r)

                finish(t, r)
                for i in range(GROUP):
                    s = r * GROUP + i
                    block = held[t, s]
                    pltpu.matmul_push_rhs(block, i % 2, 0)
                    pltpu.matmul_push_rhs(block, i % 2, 1)
                    pltpu.matmul_acc_lhs(first_sum, turned_ref[info_ref[t, slots + s]], i % 2)
                    pltpu.matmul_acc_lhs(second_sum, turned_ref[info_ref[t, 2 * slots + s]], i % 2)
                return carry

            lax.fori_loop(0, rounds, one_round, 0)
            begin_rounds(following, rounds, jnp.maximum(rounds, next_rounds))

            @pl.when(t == 0)
            def factors():
                load_parts.wait()

            rows = (
                split3(pltpu.matmul_pop(first_sum).T),
                split3(pltpu.matmul_pop(second_sum).T),
            )
            products = ((0, 0), (0, 1), (1, 0), (0, 2), (1, 1), (2, 0))

            def terms(half, columns, chosen):
                return [(rows[half][i], parts_ref[j, half, columns]) for i, j in chosen]

            multiply(first_sum, 0, terms(0, 0, products))
            multiply(second_sum, 1, terms(0, 1, products) + terms(1, 1, products[3:]))
            out_ref[t, 0] = pltpu.matmul_pop(first_sum)
            store(t, 0).start()
            multiply(first_sum, 0, terms(1, 1, products[:3]))
            out_ref[t, 1] = pltpu.matmul_pop(second_sum) + pltpu.matmul_pop(first_sum)
            store(t, 1).start()
            return carry

        lax.fori_loop(0, tiles, tile_step, 0)
        for t in range(tiles):
            for half in range(2):
                store(t, half).wait()

    pl.run_scoped(main, *sums)


def far(info, blocks, turned_near, parts):
    tiles = info.shape[0]
    slots = info.shape[1] // 3
    size = blocks.shape[1]
    hbm = pl.BlockSpec(memory_space=pltpu.HBM)
    sums = [pltpu.ACC(mxu_id=n)((size, size), jnp.float32) for n in range(2)]
    return pl.pallas_call(
        functools.partial(far_kernel, slots, sums),
        out_shape=jax.ShapeDtypeStruct((tiles * size, 2 * size), jnp.float32),
        in_specs=[pl.BlockSpec(memory_space=pltpu.SMEM), hbm, hbm, hbm],
        out_specs=hbm,
        scratch_shapes=[
            pltpu.VMEM((tiles, slots, size, size), jnp.bfloat16),
            pltpu.VMEM(turned_near.shape, jnp.bfloat16),
            pltpu.VMEM(parts.shape, jnp.bfloat16),
            pltpu.VMEM((tiles, 2, size, size), jnp.float32),
            pltpu.SemaphoreType.DMA((tiles, slots // GROUP)),
            pltpu.SemaphoreType.DMA((2,)),
            pltpu.SemaphoreType.DMA((tiles, 2)),
        ],
        compiler_params=pltpu.CompilerParams(vmem_limit_bytes=63 << 20),
        name="far",
    )(info, blocks, turned_near, parts)


def local_pairs(near_first, near_second, counts, near_total):
    slots = near_first.shape[1]
    usable = jnp.arange(slots, dtype=jnp.int32)[None, :] < counts[:, None]
    labels = jnp.arange(near_total, dtype=jnp.int32)
    first_hot = (near_first[:, :, None] == labels) & usable[:, :, None]
    second_hot = near_second[:, :, None] == labels
    both = first_hot[:, :, :, None] & second_hot[:, :, None, :]
    return jnp.sum(both.astype(jnp.float32), axis=(0, 1))


def total_pairs(value):
    for axis, bits in (("row", (1, 4, 2)), ("col", (8, 4, 2, 1))):
        size = lax.axis_size(axis)
        for bit in bits:
            value = value + lax.ppermute(value, axis, [(i, i ^ bit) for i in range(size)])
    return value


def shards(
    response_cache, near_cache, lead_diag, far_offsets, near_first, near_second, tile_counts
):
    near_total = near_cache.shape[0]
    cached, size = response_cache.shape[:2]
    share = cached * size // lax.axis_size("row")
    own = lax.dynamic_slice_in_dim(
        response_cache.reshape(cached * size, size), lax.axis_index("row") * share, share, 0
    )
    blocks = lax.all_gather(own, ("col", "row"), axis=0, tiled=True).reshape(-1, size, size)
    pairs = total_pairs(local_pairs(near_first, near_second, tile_counts, near_total))
    turned = jnp.transpose(near_cache, (0, 2, 1))
    padded = jnp.concatenate([turned, jnp.zeros_like(turned[:1])], axis=0)
    lead_factor, parts = lead(pairs, near_cache, turned, lead_diag)
    usable = jnp.arange(far_offsets.shape[1], dtype=jnp.int32)[None, :] < tile_counts[:, None]
    info = jnp.concatenate(
        [far_offsets]
        + [jnp.where(usable, labels, near_total) for labels in (near_first, near_second)]
        + [tile_counts[:, None]],
        axis=1,
    )
    far_factor = far(info, blocks, padded, parts)
    return lead_factor, far_factor


def solution(mesh):
    return jax.shard_map(
        shards,
        mesh=mesh,
        in_specs=(
            P("col", None, None),
            P(),
            P(),
            P(("row", "col"), None),
            P(("row", "col"), None),
            P(("row", "col"), None),
            P(("row", "col")),
        ),
        out_specs=(P(), P(("row", "col"), None)),
        check_vma=False,
    )
```
